512 devices in a mesh: leaf: 128 (over y, z, core), panel: 4 (over x).
Axes of the slice: x: 4, y: 4, z: 16, core: 2. Of those that a mesh axis runs over, the one named last changes fastest.
Arguments:
- border: bfloat16 [128, 128, 8192], P('leaf', 'panel'), may hold values from -0.046875 to 0.046875
- solution: bfloat16 [128, 128, 128], P('leaf', 'panel'), may hold values from -6 to 6
- winv_top: bfloat16 [4096, 4096], P(None, ('leaf', 'panel')), as said below
- winv_mid: bfloat16 [4096, 8192], P(None, ('leaf', 'panel')), as said below
- coupling: bfloat16 [8192, 4096], P(('leaf', 'panel')), may hold values from -0.0625 to 0.0625
Outputs:
- top_adjoint: float32 [4096, 128], P(('leaf', 'panel'))
- mid_adjoint: float32 [8192, 128], P(('leaf', 'panel'))
The draws below stay inside these ranges and needn't reach their ends.
Inputs may be any that keep to these rules, and one draw needn't show every extreme that they name: `winv_top`: each 4096 x 4096 block of the factor is lower triangular with a positive diagonal. `winv_mid`: each 4096 x 4096 block of the factor is lower triangular with a positive diagonal.
All inputs are finite; a program needn't handle non-finite values.
Results may differ from the reference program's by a relative error of at most 0.0003.
Values sent between devices are 32-bit elements; how exact they have to be, the bound alone decides.
A program may use at most 64 MiB of HBM per device.

```python
import math
import jax
import jax.numpy as jnp
from jax import lax

S = 4096
R = 128
K = 128
N_LEAF = 128


def lower_blocks(key, row_count, col_count):
    first_key, second_key = jax.random.split(key)
    lower_part = jax.random.normal(first_key, (row_count, col_count), jnp.float32) * (0.6 / math.sqrt(S))
    diag_part = jax.random.uniform(second_key, (row_count, col_count), jnp.float32, 0.5, 1.5)
    row_ids = jax.lax.broadcasted_iota(jnp.int32, (row_count, col_count), 0)
    col_ids = jax.lax.broadcasted_iota(jnp.int32, (row_count, col_count), 1) % S
    return jnp.where(col_ids < row_ids, lower_part, jnp.where(col_ids == row_ids, diag_part, 0.0))


def draw_winv_top(key, part):
    return lower_blocks(jax.random.fold_in(key, 11), S, S).astype(jnp.bfloat16)


def draw_winv_mid(key, part):
    return lower_blocks(jax.random.fold_in(key, 23), S, 2 * S).astype(jnp.bfloat16)


def steps_of(own_key, dims, cuts, low, largest):
    def one(position, shards_of):
        steps = jax.random.uniform(jax.random.fold_in(jax.random.fold_in(own_key, 6), position), (shards_of,), jnp.float32, low / len(cuts), largest / len(cuts))
        return jnp.repeat(jnp.exp(steps), dims[position] // shards_of).reshape((-1,) + (1,) * (len(dims) - position - 1))

    gain = one(*cuts[0])
    for cut in cuts[1:]:
        gain = gain * one(*cut)
    return gain


def gaussian(stream_key, shape, scale, bound, pieces=(), held_as=jnp.bfloat16):
    entries = jax.random.normal(stream_key, shape, jnp.float32) * scale
    if len(pieces) > 0:
        entries = steps_of(stream_key, shape, pieces, -0.22, 0.18) * entries
    return jnp.clip(entries, min=-bound, max=bound).astype(held_as)


def setup_inputs(seed: int = 0) -> dict:
    seeds = jax.random.split(jax.random.key(seed), 6)
    border = gaussian(seeds[0], (N_LEAF, K, 2 * S), (K * N_LEAF) ** -0.5, 0.046875, ((0, 128), (1, 4)))
    solution = gaussian(seeds[1], (N_LEAF, K, R), 1.0, 6.0, ((0, 128), (1, 4)))
    winv_top = draw_winv_top(jax.random.fold_in(seeds[5], 71), 0)
    winv_mid = draw_winv_mid(jax.random.fold_in(seeds[5], 71), 0)
    coupling = gaussian(seeds[4], (2 * S, S), (2 * S) ** -0.5, 0.0625, ((0, 512),))
    return dict(border=border, solution=solution, winv_top=winv_top, winv_mid=winv_mid, coupling=coupling)


def add_leaf(running, inputs):
    border_rows, leaf_solution = inputs
    term = lax.dot_general(border_rows, leaf_solution, (((0,), (0,)), ((), ())), preferred_element_type=jnp.float32)
    return running + term, None


def reference(border, solution, winv_top, winv_mid, coupling):
    half_leaves = N_LEAF // 2
    totals = []
    for group_idx in range(2):
        initial = jnp.zeros((2 * S, R), jnp.float32)
        summed, unused = lax.scan(add_leaf, initial, (border[group_idx * half_leaves:(group_idx + 1) * half_leaves], solution[group_idx * half_leaves:(group_idx + 1) * half_leaves]))
        totals.append(summed)
    top_load = totals[0][:S] + totals[1][:S]
    top_factor = winv_top.astype(jnp.float32)
    top_inner = jnp.dot(top_factor, top_load, precision=lax.Precision.HIGHEST)
    top_adjoint = jnp.dot(top_factor.T, top_inner, precision=lax.Precision.HIGHEST)
    results = []
    for group_idx in range(2):
        factor = winv_mid[:, group_idx * S:(group_idx + 1) * S].astype(jnp.float32)
        couple = coupling[group_idx * S:(group_idx + 1) * S].astype(jnp.float32)
        mid_rhs = totals[group_idx][S:] - jnp.dot(couple, top_adjoint, precision=lax.Precision.HIGHEST)
        mid_inner = jnp.dot(factor, mid_rhs, precision=lax.Precision.HIGHEST)
        results.append(jnp.dot(factor.T, mid_inner, precision=lax.Precision.HIGHEST))
    return top_adjoint, jnp.concatenate(results, 0)
```

```python
import functools

import jax
import jax.numpy as jnp
from jax import lax
from jax.experimental import pallas as pl
from jax.experimental.pallas import tpu as pltpu
from jax.sharding import PartitionSpec as P

CHIPS_Y = 4
CORES = 2
F32 = jnp.float32
BF16 = jnp.bfloat16


def dot_split(factor, value):
    high = value.astype(BF16)
    low = (value - high.astype(F32)).astype(BF16)
    return jnp.dot(factor, low, preferred_element_type=F32) + jnp.dot(
        factor, high, preferred_element_type=F32
    )


def kernel(
    dims,
    border, solution, top_factor, mid_factor, coupling,
    top_out, mid_out,
    border_send, border_land, sol_land,
    top_land, mid_land, couple_send, couple_land,
    top_y_send, top_y_land, mid_y_send, mid_y_land,
    load_send, load_land, load_own, load_all,
    inner_send, inner_land, inner_own, inner_all,
    adj_send, adj_land, adj_own, adj_all,
    rhs_send, rhs_land, rhs_own, rhs_all,
    minner_send, minner_land, minner_own, minner_all,
    madj_send, madj_land,
    send_sem, recv_sem,
):
    ny, nz, nx = dims
    nq = CORES * nx
    half = ny // 2
    leaf = lax.axis_index("leaf")
    x = lax.axis_index("panel")
    c = lax.rem(leaf, CORES)
    z = lax.rem(lax.div(leaf, CORES), nz)
    y = lax.div(leaf, CORES * nz)
    q = c * nx + x
    y_low = lax.rem(y, half)
    y_base = y - y_low

    def device(y_at, z_at, q_at):
        return ((y_at * nz + z_at) * CORES + lax.div(q_at, nx), lax.rem(q_at, nx))

    groups = {
        "q": (nq, q, lambda i: device(y, z, i)),
        "y": (ny, y, lambda i: device(i, z, q)),
        "pair": (half, y_low, lambda i: device(y_base + i, z, q)),
        "z": (nz, z, lambda i: device(y, i, q)),
        "plane": (ny * nq, y * nq + q, lambda i: device(lax.div(i, nq), z, lax.rem(i, nq))),
        "half": (
            half * nq,
            y_low * nq + q,
            lambda i: device(y_base + lax.div(i, nq), z, lax.rem(i, nq)),
        ),
    }
    pending = []

    def send(slot, group, source, landing):
        count, me, target = groups[group]

        def one(step, carry):
            peer = lax.rem(me + step, count)
            pltpu.make_async_remote_copy(
                src_ref=source(peer),
                dst_ref=landing.at[me],
                send_sem=send_sem.at[slot],
                recv_sem=recv_sem.at[slot],
                device_id=target(peer),
                device_id_type=pl.DeviceIdType.MESH,
            ).start()
            return carry

        lax.fori_loop(1, count, one, 0)
        others = landing.at[pl.ds(0, count - 1)]
        whole = pltpu.make_async_remote_copy(
            src_ref=others,
            dst_ref=others,
            send_sem=send_sem.at[slot],
            recv_sem=recv_sem.at[slot],
            device_id=target(lax.rem(me + 1, count)),
            device_id_type=pl.DeviceIdType.MESH,
        )
        pending.append(whole)
        return whole

    def scatter_sum(slot, group, buffer, landing):
        me = groups[group][1]
        whole = send(slot, group, lambda peer: buffer.at[peer], landing)
        landing[me] = buffer[me]
        whole.wait_recv()
        return jnp.sum(landing[...], axis=0)

    def gather(slot, group, own, landing):
        me = groups[group][1]
        whole = send(slot, group, lambda peer: own, landing)
        landing[me] = own[...]
        whole.wait_recv()
        value = landing[...]
        return value.reshape(-1, value.shape[-1])

    barrier = pltpu.get_barrier_semaphore()
    for name in ("plane", "z"):
        count, me, target = groups[name]

        def greet(step, carry, count=count, me=me, target=target):
            pl.semaphore_signal(
                barrier,
                inc=1,
                device_id=target(lax.rem(me + step, count)),
                device_id_type=pl.DeviceIdType.MESH,
            )
            return carry

        lax.fori_loop(1, count, greet, 0)

    rows = border.shape[0]
    top_rows = top_out.shape[0]
    mid_rows = mid_out.shape[0]
    block = nz * nq * top_rows
    lanes = nz * top_rows
    source_id = lax.broadcasted_iota(jnp.int32, (block, lanes), 0)
    lane_id = lax.broadcasted_iota(jnp.int32, (block, lanes), 1)
    for part, owned in ((0, top_rows), (1, mid_rows)):
        first = part * ny
        stacked = jnp.concatenate(
            [border[:, (first + b) * block : (first + b + 1) * block] for b in range(ny)], 0
        )
        offset = source_id - (
            lax.div(lane_id, owned) * (nq * owned) + lax.rem(lane_id, owned)
        )

        def pick(at, carry, stacked=stacked, offset=offset, owned=owned, first=first):
            chosen = jnp.where(offset == at * owned, 1.0, 0.0).astype(BF16)
            moved = jnp.dot(stacked, chosen, preferred_element_type=F32)
            border_send[at, pl.ds(first, ny)] = moved.reshape(ny, rows, lanes)
            return carry

        lax.fori_loop(0, nq, pick, 0)

    seg = nq * top_rows
    low_half = lax.broadcasted_iota(jnp.int32, (mid_rows, 2 * seg), 1) < seg
    for z_at in range(nz):
        for pair in range(ny // 2):
            tiles = []
            for y_at in (2 * pair, 2 * pair + 1):
                start = (y_at * nz + z_at - z_at % 2) * seg
                tiles.append(coupling[:, start : start + 2 * seg].astype(F32))
            if z_at % 2 == 0:
                tiles[1] = pltpu.roll(tiles[1], seg, 1)
            else:
                tiles[0] = pltpu.roll(tiles[0], seg, 1)
            couple_send[z_at, :, pair * 2 * seg : (pair + 1) * 2 * seg] = jnp.where(
                low_half, tiles[0], tiles[1]
            )

    pl.semaphore_wait(barrier, ny * nq + nz - 2)

    sol_wait = send(0, "q", lambda peer: solution, sol_land)
    border_wait = send(1, "q", lambda peer: border_send.at[peer], border_land)
    width = top_factor.shape[1] // nz

    def columns(ref):
        return lambda peer: ref.at[:, pl.ds(pl.multiple_of(peer * width, width), width)]

    top_wait = send(2, "z", columns(top_factor), top_land)
    couple_wait = send(3, "z", lambda peer: couple_send.at[peer], couple_land)
    mid_wait = send(4, "z", columns(mid_factor), mid_land)
    sol_land[q] = solution[...]
    border_land[q] = border_send[q]
    own_columns = pl.ds(pl.multiple_of(z * width, width), width)
    top_land[z] = top_factor[:, own_columns]
    mid_land[z] = mid_factor[:, own_columns]
    couple_land[z] = couple_send[z]

    sol_wait.wait_recv()
    border_wait.wait_recv()
    loads = sol_land[...].reshape(nq * rows, -1).astype(BF16)

    def load_block(b):
        part = border_land[:, b].reshape(nq * rows, lanes)
        return jnp.dot(part.T.astype(BF16), loads, preferred_element_type=F32)

    for b in range(ny):
        top_y_send[b] = load_block(b)
    per_half = ny // half
    top_y_wait = send(5, "y", lambda peer: top_y_send.at[peer], top_y_land)
    for b in range(ny):
        mid_y_send[b // per_half, (b % per_half) * lanes : (b % per_half + 1) * lanes] = load_block(
            ny + b
        )
    mid_y_wait = send(6, "pair", lambda peer: mid_y_send.at[peer], mid_y_land)
    top_y_land[y] = top_y_send[y]
    mid_y_land[y_low] = mid_y_send[y_low]

    top_wait.wait_recv()
    top_t = top_land[...].reshape(nz * top_rows, width)
    top_w = top_t.T.astype(BF16)
    top_t = top_t.astype(BF16)

    top_y_wait.wait_recv()
    load_send[...] = jnp.sum(top_y_land[...], axis=0).reshape(load_send.shape)
    load_own[...] = scatter_sum(7, "z", load_send, load_land)
    top_load = gather(8, "z", load_own, load_all)

    inner_send[...] = dot_split(top_w, top_load).reshape(inner_send.shape)
    inner_own[...] = scatter_sum(9, "plane", inner_send, inner_land)
    top_inner = gather(10, "plane", inner_own, inner_all)

    adj_send[...] = dot_split(top_t, top_inner).reshape(adj_send.shape)
    adjoint = scatter_sum(11, "z", adj_send, adj_land)
    adj_own[...] = adjoint
    top_out[...] = adjoint
    top_block = gather(12, "plane", adj_own, adj_all)

    couple_wait.wait_recv()
    couple = couple_land[...].reshape(nz * mid_rows, width).astype(BF16)
    mid_y_wait.wait_recv()
    mid_load = jnp.sum(mid_y_land[...], axis=0)
    rhs_send[...] = (mid_load - dot_split(couple, top_block)).reshape(rhs_send.shape)
    rhs_own[...] = scatter_sum(13, "z", rhs_send, rhs_land)
    mid_wait.wait_recv()
    mid_t = mid_land[...].reshape(nz * mid_rows, width)
    mid_w = mid_t.T.astype(BF16)
    mid_t = mid_t.astype(BF16)
    mid_rhs = gather(14, "z", rhs_own, rhs_all)

    minner_send[...] = dot_split(mid_w, mid_rhs).reshape(minner_send.shape)
    minner_own[...] = scatter_sum(15, "half", minner_send, minner_land)
    mid_inner = gather(16, "half", minner_own, minner_all)

    madj_send[...] = dot_split(mid_t, mid_inner).reshape(madj_send.shape)
    mid_out[...] = scatter_sum(17, "z", madj_send, madj_land)

    for whole in pending:
        whole.wait_send()


def body(dims, border, solution, winv_top, winv_mid, coupling):
    ny, nz, nx = dims
    nq = CORES * nx
    half = ny // 2
    rows, width = border.shape[1:]
    loads = solution.shape[2]
    top_rows = winv_top.shape[1]
    mid_rows = winv_mid.shape[1]
    front = winv_top.shape[0]
    z_width = front // nz

    def buf(*shape):
        return pltpu.VMEM(shape, F32)

    def exchange(count, height):
        return [buf(count, height, loads), buf(count, height, loads)]

    def reduce_gather(count, height):
        return exchange(count, height) + [buf(height, loads), buf(count, height, loads)]

    plane = ny * nq
    scratch = (
        [buf(nq, 2 * ny, rows, nz * top_rows)] * 2
        + [buf(nq, rows, loads)]
        + [buf(nz, top_rows, z_width), buf(nz, mid_rows, z_width)]
        + [buf(nz, mid_rows, z_width)] * 2
        + exchange(ny, nz * top_rows)
        + exchange(half, nz * mid_rows)
        + reduce_gather(nz, top_rows)
        + reduce_gather(plane, z_width // plane)
        + [buf(nz, top_rows, loads)] * 2
        + [buf(top_rows, loads), buf(plane, top_rows, loads)]
        + reduce_gather(nz, mid_rows)
        + reduce_gather(half * nq, z_width // (half * nq))
        + exchange(nz, mid_rows)
        + [pltpu.SemaphoreType.DMA((18,)), pltpu.SemaphoreType.DMA((18,))]
    )
    vmem = pl.BlockSpec(memory_space=pltpu.VMEM)
    return pl.pallas_call(
        functools.partial(kernel, dims),
        out_shape=(
            jax.ShapeDtypeStruct((top_rows, loads), F32),
            jax.ShapeDtypeStruct((mid_rows, loads), F32),
        ),
        in_specs=[vmem] * 5,
        out_specs=(vmem, vmem),
        scratch_shapes=scratch,
        compiler_params=pltpu.CompilerParams(collective_id=0, has_side_effects=True),
        name="adjoint",
    )(
        border[0],
        solution[0].astype(F32),
        winv_top.T.astype(F32),
        winv_mid.T.astype(F32),
        coupling,
    )


def solution(mesh, chips_y=CHIPS_Y):
    placed = (
        P("leaf", "panel", None),
        P("leaf", "panel", None),
        P(None, ("leaf", "panel")),
        P(None, ("leaf", "panel")),
        P(("leaf", "panel"), None),
    )
    dims = (chips_y, mesh.shape["leaf"] // (CORES * chips_y), mesh.shape["panel"])
    return jax.shard_map(
        functools.partial(body, dims),
        mesh=mesh,
        in_specs=placed,
        out_specs=(P(("leaf", "panel"), None), P(("leaf", "panel"), None)),
        check_vma=False,
    )
```

```python
import functools

import jax
import jax.numpy as jnp
from jax import lax
from jax.experimental import pallas as pl
from jax.experimental.pallas import tpu as pltpu
from jax.sharding import PartitionSpec as P

CHIPS_Y = 4
CORES = 2
F32 = jnp.float32
BF16 = jnp.bfloat16


def dot_split(factor, value):
    high = value.astype(BF16)
    low = (value - high.astype(F32)).astype(BF16)
    return jnp.dot(factor, low, preferred_element_type=F32) + jnp.dot(
        factor, high, preferred_element_type=F32
    )


def kernel(
    dims,
    border, solution, top_factor, mid_factor, coupling,
    top_out, mid_out,
    border_send, border_land, sol_send, sol_land, sol_blocks,
    top_send, top_land, mid_send, mid_land, couple_send, couple_land,
    top_y_send, top_y_land, mid_y_send, mid_y_land,
    load_send, load_land, load_own, load_all,
    inner_send, inner_land, inner_own, inner_all,
    adj_send, adj_land, adj_own, adj_all,
    rhs_send, rhs_land, rhs_own, rhs_all,
    minner_send, minner_land, minner_own, minner_all,
    madj_send, madj_land,
    send_sem, recv_sem,
):
    ny, nz, nx = dims
    nq = CORES * nx
    half = ny // 2
    leaf = lax.axis_index("leaf")
    x = lax.axis_index("panel")
    c = lax.rem(leaf, CORES)
    z = lax.rem(lax.div(leaf, CORES), nz)
    y = lax.div(leaf, CORES * nz)
    q = c * nx + x
    y_low = lax.rem(y, half)
    y_base = y - y_low

    def device(y_at, z_at, q_at):
        return ((y_at * nz + z_at) * CORES + lax.div(q_at, nx), lax.rem(q_at, nx))

    groups = {
        "q": (nq, q, lambda i: device(y, z, i)),
        "y": (ny, y, lambda i: device(i, z, q)),
        "pair": (half, y_low, lambda i: device(y_base + i, z, q)),
        "z": (nz, z, lambda i: device(y, i, q)),
        "plane": (ny * nq, y * nq + q, lambda i: device(lax.div(i, nq), z, lax.rem(i, nq))),
        "half": (
            half * nq,
            y_low * nq + q,
            lambda i: device(y_base + lax.div(i, nq), z, lax.rem(i, nq)),
        ),
    }
    pending = []

    def send(slot, group, source, landing):
        count, me, target = groups[group]

        def one(step, carry):
            peer = lax.rem(me + step, count)
            pltpu.make_async_remote_copy(
                src_ref=source(peer),
                dst_ref=landing.at[me],
                send_sem=send_sem.at[slot],
                recv_sem=recv_sem.at[slot],
                device_id=target(peer),
                device_id_type=pl.DeviceIdType.MESH,
            ).start()
            return carry

        lax.fori_loop(1, count, one, 0)
        others = landing.at[pl.ds(0, count - 1)]
        whole = pltpu.make_async_remote_copy(
            src_ref=others,
            dst_ref=others,
            send_sem=send_sem.at[slot],
            recv_sem=recv_sem.at[slot],
            device_id=target(lax.rem(me + 1, count)),
            device_id_type=pl.DeviceIdType.MESH,
        )
        pending.append(whole)
        return whole

    def scatter_sum(slot, group, buffer, landing):
        me = groups[group][1]
        whole = send(slot, group, lambda peer: buffer.at[peer], landing)
        landing[me] = buffer[me]
        whole.wait_recv()
        return jnp.sum(landing[...], axis=0)

    def gather(slot, group, own, landing):
        me = groups[group][1]
        whole = send(slot, group, lambda peer: own, landing)
        landing[me] = own[...]
        whole.wait_recv()
        value = landing[...]
        return value.reshape(-1, value.shape[-1])

    barrier = pltpu.get_barrier_semaphore()
    for name in ("plane", "z"):
        count, me, target = groups[name]

        def greet(step, carry, count=count, me=me, target=target):
            pl.semaphore_signal(
                barrier,
                inc=1,
                device_id=target(lax.rem(me + step, count)),
                device_id_type=pl.DeviceIdType.MESH,
            )
            return carry

        lax.fori_loop(1, count, greet, 0)

    rows = border.shape[0]
    top_rows = top_out.shape[0]
    mid_rows = mid_out.shape[0]
    block = nz * nq * top_rows
    lanes = nz * top_rows
    width = top_factor.shape[1] // nz
    sol_send[...] = solution[...].astype(F32)
    top_send[...] = top_factor[...].astype(F32)
    for part, owned in ((0, top_rows), (1, mid_rows)):
        first = part * ny
        stacked = jnp.concatenate(
            [border[:, (first + b) * block : (first + b + 1) * block] for b in range(ny)], 0
        )
        turned = stacked.astype(F32).T.reshape(block // (nq * owned), nq, owned, ny * rows)
        for q_at in range(nq):
            border_send[q_at, part] = turned[:, q_at].reshape(lanes, ny * rows)
    sol_blocks[...] = jnp.zeros_like(sol_blocks)

    pl.semaphore_wait(barrier, ny * nq + nz - 2)

    def columns(ref):
        return lambda peer: ref.at[:, pl.ds(pl.multiple_of(peer * width, width), width)]

    own_columns = pl.ds(pl.multiple_of(z * width, width), width)
    sol_wait = send(0, "q", lambda peer: sol_send, sol_land)
    border_wait = send(1, "q", lambda peer: border_send.at[peer], border_land)
    top_wait = send(2, "z", columns(top_send), top_land)
    sol_land[q] = sol_send[...]
    border_land[q] = border_send[q]
    top_land[z] = top_send[:, own_columns]

    seg = nq * top_rows
    low_half = lax.broadcasted_iota(jnp.int32, (mid_rows, 2 * seg), 1) < seg
    for z_at in range(nz):
        for pair in range(ny // 2):
            tiles = []
            for y_at in (2 * pair, 2 * pair + 1):
                start = (y_at * nz + z_at - z_at % 2) * seg
                tiles.append(coupling[:, start : start + 2 * seg].astype(F32))
            if z_at % 2 == 0:
                tiles[1] = pltpu.roll(tiles[1], seg, 1)
            else:
                tiles[0] = pltpu.roll(tiles[0], seg, 1)
            couple_send[z_at, :, pair * 2 * seg : (pair + 1) * 2 * seg] = jnp.where(
                low_half, tiles[0], tiles[1]
            )

    couple_wait = send(3, "z", lambda peer: couple_send.at[peer], couple_land)
    couple_land[z] = couple_send[z]
    mid_send[...] = mid_factor[...].astype(F32)
    mid_land[z] = mid_send[:, own_columns]

    sol_wait.wait_recv()
    columns_out = sol_send.shape[1]
    for source in range(nq):
        part = sol_land[source].astype(BF16)
        for b in range(ny):
            sol_blocks[
                source,
                b * rows : (b + 1) * rows,
                b * columns_out : (b + 1) * columns_out,
            ] = part
    border_wait.wait_recv()

    def loads(part):
        total = None
        for source in range(0, nq, 2):
            left = jnp.concatenate(
                [border_land[source, part], border_land[source + 1, part]], 1
            ).astype(BF16)
            right = sol_blocks[source : source + 2].reshape(2 * ny * rows, -1)
            term = jnp.dot(left, right, preferred_element_type=F32)
            total = term if total is None else total + term
        return [total[:, b * columns_out : (b + 1) * columns_out] for b in range(ny)]

    for b, value in enumerate(loads(0)):
        top_y_send[b] = value
    per_half = ny // half
    top_y_wait = send(5, "y", lambda peer: top_y_send.at[peer], top_y_land)
    for b, value in enumerate(loads(1)):
        mid_y_send[b // per_half, (b % per_half) * lanes : (b % per_half + 1) * lanes] = value
    mid_y_wait = send(6, "pair", lambda peer: mid_y_send.at[peer], mid_y_land)
    top_y_land[y] = top_y_send[y]
    mid_y_land[y_low] = mid_y_send[y_low]

    top_wait.wait_recv()
    top_t = top_land[...].reshape(nz * top_rows, width)
    top_w = top_t.T.astype(BF16)
    top_t = top_t.astype(BF16)

    top_y_wait.wait_recv()
    load_send[...] = jnp.sum(top_y_land[...], axis=0).reshape(load_send.shape)
    load_own[...] = scatter_sum(7, "z", load_send, load_land)
    top_load = gather(8, "z", load_own, load_all)
    mid_wait = send(4, "z", columns(mid_send), mid_land)

    inner_send[...] = dot_split(top_w, top_load).reshape(inner_send.shape)
    inner_own[...] = scatter_sum(9, "plane", inner_send, inner_land)
    top_inner = gather(10, "plane", inner_own, inner_all)

    adj_send[...] = dot_split(top_t, top_inner).reshape(adj_send.shape)
    adjoint = scatter_sum(11, "z", adj_send, adj_land)
    adj_own[...] = adjoint
    top_out[...] = adjoint
    top_block = gather(12, "plane", adj_own, adj_all)

    couple_wait.wait_recv()
    couple = couple_land[...].reshape(nz * mid_rows, width).astype(BF16)
    mid_y_wait.wait_recv()
    mid_load = jnp.sum(mid_y_land[...], axis=0)
    rhs_send[...] = (mid_load - dot_split(couple, top_block)).reshape(rhs_send.shape)
    rhs_own[...] = scatter_sum(13, "z", rhs_send, rhs_land)
    mid_wait.wait_recv()
    mid_t = mid_land[...].reshape(nz * mid_rows, width)
    mid_w = mid_t.T.astype(BF16)
    mid_t = mid_t.astype(BF16)
    mid_rhs = gather(14, "z", rhs_own, rhs_all)

    minner_send[...] = dot_split(mid_w, mid_rhs).reshape(minner_send.shape)
    minner_own[...] = scatter_sum(15, "half", minner_send, minner_land)
    mid_inner = gather(16, "half", minner_own, minner_all)

    madj_send[...] = dot_split(mid_t, mid_inner).reshape(madj_send.shape)
    mid_out[...] = scatter_sum(17, "z", madj_send, madj_land)

    for whole in pending:
        whole.wait_send()


def body(dims, border, solution, winv_top, winv_mid, coupling):
    ny, nz, nx = dims
    nq = CORES * nx
    half = ny // 2
    rows, width = border.shape[1:]
    loads = solution.shape[2]
    top_rows = winv_top.shape[1]
    mid_rows = winv_mid.shape[1]
    front = winv_top.shape[0]
    z_width = front // nz

    def buf(*shape):
        return pltpu.VMEM(shape, F32)

    def exchange(count, height):
        return [buf(count, height, loads), buf(count, height, loads)]

    def reduce_gather(count, height):
        return exchange(count, height) + [buf(height, loads), buf(count, height, loads)]

    plane = ny * nq
    scratch = (
        [buf(nq, 2, nz * top_rows, ny * rows)] * 2
        + [buf(rows, loads), buf(nq, rows, loads)]
        + [pltpu.VMEM((nq, ny * rows, ny * loads), BF16)]
        + [buf(top_rows, front), buf(nz, top_rows, z_width)]
        + [buf(mid_rows, front), buf(nz, mid_rows, z_width)]
        + [buf(nz, mid_rows, z_width)] * 2
        + exchange(ny, nz * top_rows)
        + exchange(half, nz * mid_rows)
        + reduce_gather(nz, top_rows)
        + reduce_gather(plane, z_width // plane)
        + [buf(nz, top_rows, loads)] * 2
        + [buf(top_rows, loads), buf(plane, top_rows, loads)]
        + reduce_gather(nz, mid_rows)
        + reduce_gather(half * nq, z_width // (half * nq))
        + exchange(nz, mid_rows)
        + [pltpu.SemaphoreType.DMA((18,)), pltpu.SemaphoreType.DMA((18,))]
    )
    vmem = pl.BlockSpec(memory_space=pltpu.VMEM)
    return pl.pallas_call(
        functools.partial(kernel, dims),
        out_shape=(
            jax.ShapeDtypeStruct((top_rows, loads), F32),
            jax.ShapeDtypeStruct((mid_rows, loads), F32),
        ),
        in_specs=[vmem] * 5,
        out_specs=(vmem, vmem),
        scratch_shapes=scratch,
        compiler_params=pltpu.CompilerParams(collective_id=0, has_side_effects=True),
        name="adjoint",
    )(
        border[0],
        solution[0],
        winv_top.T,
        winv_mid.T,
        coupling,
    )


def solution(mesh, chips_y=CHIPS_Y):
    placed = (
        P("leaf", "panel", None),
        P("leaf", "panel", None),
        P(None, ("leaf", "panel")),
        P(None, ("leaf", "panel")),
        P(("leaf", "panel"), None),
    )
    dims = (chips_y, mesh.shape["leaf"] // (CORES * chips_y), mesh.shape["panel"])
    return jax.shard_map(
        functools.partial(body, dims),
        mesh=mesh,
        in_specs=placed,
        out_specs=(P(("leaf", "panel"), None), P(("leaf", "panel"), None)),
        check_vma=False,
    )
```

```python
import functools

import jax
import jax.numpy as jnp
from jax import lax
from jax.experimental import pallas as pl
from jax.experimental.pallas import tpu as pltpu
from jax.sharding import PartitionSpec as P

CHIPS_Y = 4
CORES = 2
F32 = jnp.float32
BF16 = jnp.bfloat16


def dot_split(factor, value):
    high = value.astype(BF16)
    low = (value - high.astype(F32)).astype(BF16)
    return jnp.dot(factor, low, preferred_element_type=F32) + jnp.dot(
        factor, high, preferred_element_type=F32
    )


def kernel(
    dims,
    border, solution, top_factor, mid_factor, coupling,
    top_out, mid_out,
    border_send, border_land, sol_send, sol_land, sol_blocks,
    top_send, top_land, mid_send, mid_land, couple_send, couple_land,
    top_y_send, top_y_land, mid_y_send, mid_y_land,
    load_send, load_land, load_own, load_all,
    inner_send, inner_land, inner_own, inner_all,
    adj_send, adj_land, adj_own, adj_all,
    rhs_send, rhs_land, rhs_own, rhs_all,
    minner_send, minner_land, minner_own, minner_all,
    madj_send, madj_land,
    send_sem, recv_sem,
):
    ny, nz, nx = dims
    nq = CORES * nx
    half = ny // 2
    leaf = lax.axis_index("leaf")
    x = lax.axis_index("panel")
    c = lax.rem(leaf, CORES)
    z = lax.rem(lax.div(leaf, CORES), nz)
    y = lax.div(leaf, CORES * nz)
    q = c * nx + x
    y_low = lax.rem(y, half)
    y_base = y - y_low

    def ring(me, count):
        steps = sorted(range(1, count), key=lambda step: -min(step, count - step))
        return [lax.rem(me + step, count) for step in steps]

    def leaf_of(y_at, z_at, c_at):
        return (y_at * nz + z_at) * CORES + c_at

    xs, zs, ys, lows = ring(x, nx), ring(z, nz), ring(y, ny), ring(y_low, half)
    flips = [1 - c]

    def sheet(me, others, base):
        return [
            (y_at * nq + c_at * nx + x_at, (leaf_of(base + y_at, z, c_at), x_at))
            for y_at in others + [me]
            for x_at in xs + [x]
            for c_at in flips + [c]
        ][:-1]

    groups = {
        "q": (nq, q, [(c_at * nx + x_at, (leaf_of(y, z, c_at), x_at)) for x_at in xs + [x] for c_at in flips + [c]][:-1]),
        "y": (ny, y, [(y_at, (leaf_of(y_at, z, c), x)) for y_at in ys]),
        "pair": (half, y_low, [(low, (leaf_of(y_base + low, z, c), x)) for low in lows]),
        "z": (nz, z, [(z_at, (leaf_of(y, z_at, c), x)) for z_at in zs]),
        "plane": (ny * nq, y * nq + q, sheet(y, ys, 0)),
        "half": (half * nq, y_low * nq + q, sheet(y_low, lows, y_base)),
    }
    pending = []

    def push(slot, group, source, landing, peers):
        me = groups[group][1]
        for peer, target in peers:
            pltpu.make_async_remote_copy(
                src_ref=source(peer),
                dst_ref=landing.at[me],
                send_sem=send_sem.at[slot],
                recv_sem=recv_sem.at[slot],
                device_id=target,
                device_id_type=pl.DeviceIdType.MESH,
            ).start()

    def waiter(slot, group, landing):
        count, me, peers = groups[group]
        others = landing.at[pl.ds(0, count - 1)]
        whole = pltpu.make_async_remote_copy(
            src_ref=others,
            dst_ref=others,
            send_sem=send_sem.at[slot],
            recv_sem=recv_sem.at[slot],
            device_id=peers[0][1],
            device_id_type=pl.DeviceIdType.MESH,
        )
        pending.append(whole)
        return whole

    def send(slot, group, source, landing):
        push(slot, group, source, landing, groups[group][2])
        return waiter(slot, group, landing)

    def scatter_sum(slot, group, buffer, landing, between=None):
        me = groups[group][1]
        whole = send(slot, group, lambda peer: buffer.at[peer], landing)
        landing[me] = buffer[me]
        if between is not None:
            between()
        whole.wait_recv()
        return jnp.sum(landing[...], axis=0)

    def gather(slot, group, own, landing, between=None):
        me = groups[group][1]
        whole = send(slot, group, lambda peer: own, landing)
        landing[me] = own[...]
        if between is not None:
            between()
        whole.wait_recv()
        value = landing[...]
        return value.reshape(-1, value.shape[-1])

    barrier = pltpu.get_barrier_semaphore()
    for name in ("z", "plane"):
        for peer, target in groups[name][2]:
            pl.semaphore_signal(
                barrier, inc=1, device_id=target, device_id_type=pl.DeviceIdType.MESH
            )

    rows = border.shape[0]
    top_rows = top_out.shape[0]
    mid_rows = mid_out.shape[0]
    block = nz * nq * top_rows
    lanes = nz * top_rows
    width = top_factor.shape[1] // nz
    sol_send[...] = solution[...].astype(F32)
    top_send[...] = top_factor[...].astype(F32)

    def regroup(part, owned):
        first = part * ny
        stacked = jnp.concatenate(
            [border[:, (first + b) * block : (first + b + 1) * block] for b in range(ny)], 0
        )
        turned = stacked.astype(F32).T.reshape(block // (nq * owned), nq, owned, ny * rows)
        for q_at in range(nq):
            border_send[part, q_at] = turned[:, q_at].reshape(lanes, ny * rows)

    regroup(0, top_rows)
    pl.semaphore_wait(barrier, ny * nq + nz - 2)

    def columns(ref):
        return lambda peer: ref.at[:, pl.ds(pl.multiple_of(peer * width, width), width)]

    own_columns = pl.ds(pl.multiple_of(z * width, width), width)
    sol_wait = send(0, "q", lambda peer: sol_send, sol_land)
    border_wait = send(1, "q", lambda peer: border_send.at[0, peer], border_land.at[0])
    near = groups["z"][2][::-1]
    early, late = near[: 2 * len(near) // 3], near[2 * len(near) // 3 :]
    push(2, "z", columns(top_send), top_land, near)
    top_wait = waiter(2, "z", top_land)
    regroup(1, mid_rows)
    border_mid_wait = send(18, "q", lambda peer: border_send.at[1, peer], border_land.at[1])
    sol_land[q] = sol_send[...]
    border_land[0, q] = border_send[0, q]
    border_land[1, q] = border_send[1, q]
    sol_blocks[...] = jnp.zeros_like(sol_blocks)
    top_land[z] = top_send[:, own_columns]

    seg = nq * top_rows
    low_half = lax.broadcasted_iota(jnp.int32, (mid_rows, 2 * seg), 1) < seg
    for z_at in range(nz):
        for pair in range(ny // 2):
            tiles = []
            for y_at in (2 * pair, 2 * pair + 1):
                start = (y_at * nz + z_at - z_at % 2) * seg
                tiles.append(coupling[:, start : start + 2 * seg].astype(F32))
            if z_at % 2 == 0:
                tiles[1] = pltpu.roll(tiles[1], seg, 1)
            else:
                tiles[0] = pltpu.roll(tiles[0], seg, 1)
            couple_send[z_at, :, pair * 2 * seg : (pair + 1) * 2 * seg] = jnp.where(
                low_half, tiles[0], tiles[1]
            )

    couple_rows = lambda peer: couple_send.at[peer]
    push(3, "z", couple_rows, couple_land, early)
    couple_wait = waiter(3, "z", couple_land)
    couple_land[z] = couple_send[z]
    mid_send[...] = mid_factor[...].astype(F32)
    mid_land[z] = mid_send[:, own_columns]

    sol_wait.wait_recv()
    columns_out = sol_send.shape[1]
    for source in range(nq):
        part = sol_land[source].astype(BF16)
        for b in range(ny):
            sol_blocks[
                source,
                b * rows : (b + 1) * rows,
                b * columns_out : (b + 1) * columns_out,
            ] = part
    border_wait.wait_recv()

    def loads(part):
        total = None
        for source in range(0, nq, 2):
            left = jnp.concatenate(
                [border_land[part, source], border_land[part, source + 1]], 1
            ).astype(BF16)
            right = sol_blocks[source : source + 2].reshape(2 * ny * rows, -1)
            term = jnp.dot(left, right, preferred_element_type=F32)
            total = term if total is None else total + term
        return [total[:, b * columns_out : (b + 1) * columns_out] for b in range(ny)]

    for b, value in enumerate(loads(0)):
        top_y_send[b] = value
    per_half = ny // half
    top_y_wait = send(5, "y", lambda peer: top_y_send.at[peer], top_y_land)
    top_y_land[y] = top_y_send[y]

    def mid_loads():
        border_mid_wait.wait_recv()
        for b, value in enumerate(loads(1)):
            mid_y_send[
                b // per_half, (b % per_half) * lanes : (b % per_half + 1) * lanes
            ] = value
        push(6, "pair", lambda peer: mid_y_send.at[peer], mid_y_land, groups["pair"][2])
        mid_y_land[y_low] = mid_y_send[y_low]

    mid_y_wait = waiter(6, "pair", mid_y_land)

    def factors_early():
        push(3, "z", couple_rows, couple_land, late)
        push(4, "z", columns(mid_send), mid_land, early)

    def factors_late():
        push(4, "z", columns(mid_send), mid_land, late)

    mid_wait = waiter(4, "z", mid_land)

    top_wait.wait_recv()
    top_t = top_land[...].reshape(nz * top_rows, width)
    top_w = top_t.T.astype(BF16)
    top_t = top_t.astype(BF16)

    top_y_wait.wait_recv()
    load_send[...] = jnp.sum(top_y_land[...], axis=0).reshape(load_send.shape)
    load_own[...] = scatter_sum(7, "z", load_send, load_land)
    top_load = gather(8, "z", load_own, load_all, mid_loads)

    inner_send[...] = dot_split(top_w, top_load).reshape(inner_send.shape)
    inner_own[...] = scatter_sum(9, "plane", inner_send, inner_land, factors_early)
    top_inner = gather(10, "plane", inner_own, inner_all)

    adj_send[...] = dot_split(top_t, top_inner).reshape(adj_send.shape)
    adjoint = scatter_sum(11, "z", adj_send, adj_land)
    adj_own[...] = adjoint
    top_out[...] = adjoint
    top_block = gather(12, "plane", adj_own, adj_all, factors_late)

    couple_wait.wait_recv()
    couple = couple_land[...].reshape(nz * mid_rows, width).astype(BF16)
    mid_y_wait.wait_recv()
    mid_load = jnp.sum(mid_y_land[...], axis=0)
    rhs_send[...] = (mid_load - dot_split(couple, top_block)).reshape(rhs_send.shape)
    rhs_own[...] = scatter_sum(13, "z", rhs_send, rhs_land)
    mid_wait.wait_recv()
    mid_t = mid_land[...].reshape(nz * mid_rows, width)
    mid_w = mid_t.T.astype(BF16)
    mid_t = mid_t.astype(BF16)
    mid_rhs = gather(14, "z", rhs_own, rhs_all)

    minner_send[...] = dot_split(mid_w, mid_rhs).reshape(minner_send.shape)
    minner_own[...] = scatter_sum(15, "half", minner_send, minner_land)
    mid_inner = gather(16, "half", minner_own, minner_all)

    madj_send[...] = dot_split(mid_t, mid_inner).reshape(madj_send.shape)
    mid_out[...] = scatter_sum(17, "z", madj_send, madj_land)

    for whole in pending:
        whole.wait_send()


def body(dims, border, solution, winv_top, winv_mid, coupling):
    ny, nz, nx = dims
    nq = CORES * nx
    half = ny // 2
    rows, width = border.shape[1:]
    loads = solution.shape[2]
    top_rows = winv_top.shape[1]
    mid_rows = winv_mid.shape[1]
    front = winv_top.shape[0]
    z_width = front // nz

    def buf(*shape):
        return pltpu.VMEM(shape, F32)

    def exchange(count, height):
        return [buf(count, height, loads), buf(count, height, loads)]

    def reduce_gather(count, height):
        return exchange(count, height) + [buf(height, loads), buf(count, height, loads)]

    plane = ny * nq
    scratch = (
        [buf(2, nq, nz * top_rows, ny * rows)] * 2
        + [buf(rows, loads), buf(nq, rows, loads)]
        + [pltpu.VMEM((nq, ny * rows, ny * loads), BF16)]
        + [buf(top_rows, front), buf(nz, top_rows, z_width)]
        + [buf(mid_rows, front), buf(nz, mid_rows, z_width)]
        + [buf(nz, mid_rows, z_width)] * 2
        + exchange(ny, nz * top_rows)
        + exchange(half, nz * mid_rows)
        + reduce_gather(nz, top_rows)
        + reduce_gather(plane, z_width // plane)
        + [buf(nz, top_rows, loads)] * 2
        + [buf(top_rows, loads), buf(plane, top_rows, loads)]
        + reduce_gather(nz, mid_rows)
        + reduce_gather(half * nq, z_width // (half * nq))
        + exchange(nz, mid_rows)
        + [pltpu.SemaphoreType.DMA((19,)), pltpu.SemaphoreType.DMA((19,))]
    )
    vmem = pl.BlockSpec(memory_space=pltpu.VMEM)
    return pl.pallas_call(
        functools.partial(kernel, dims),
        out_shape=(
            jax.ShapeDtypeStruct((top_rows, loads), F32),
            jax.ShapeDtypeStruct((mid_rows, loads), F32),
        ),
        in_specs=[vmem] * 5,
        out_specs=(vmem, vmem),
        scratch_shapes=scratch,
        compiler_params=pltpu.CompilerParams(collective_id=0, has_side_effects=True),
        name="adjoint",
    )(
        border[0],
        solution[0],
        winv_top.T,
        winv_mid.T,
        coupling,
    )


def solution(mesh, chips_y=CHIPS_Y):
    placed = (
        P("leaf", "panel", None),
        P("leaf", "panel", None),
        P(None, ("leaf", "panel")),
        P(None, ("leaf", "panel")),
        P(("leaf", "panel"), None),
    )
    dims = (chips_y, mesh.shape["leaf"] // (CORES * chips_y), mesh.shape["panel"])
    return jax.shard_map(
        functools.partial(body, dims),
        mesh=mesh,
        in_specs=placed,
        out_specs=(P(("leaf", "panel"), None), P(("leaf", "panel"), None)),
        check_vma=False,
    )
```

```python
import functools

import jax
import jax.numpy as jnp
from jax import lax
from jax.experimental import pallas as pl
from jax.experimental.pallas import tpu as pltpu
from jax.sharding import PartitionSpec as P

CHIPS_Y = 4
CORES = 2
F32 = jnp.float32
BF16 = jnp.bfloat16


def dot_split(factor, value):
    high = value.astype(BF16)
    low = (value - high.astype(F32)).astype(BF16)
    return jnp.dot(factor, low, preferred_element_type=F32) + jnp.dot(
        factor, high, preferred_element_type=F32
    )


def kernel(
    dims,
    border, solution, top_factor, mid_factor, coupling,
    top_out, mid_out,
    border_send, border_land, sol_send, sol_land, sol_blocks,
    top_send, top_land, mid_send, mid_land, couple_send, couple_land,
    top_y_send, top_y_land, mid_y_send, mid_y_land,
    load_send, load_land, load_own, load_all,
    inner_send, inner_land, inner_own, inner_all,
    adj_send, adj_land, adj_own, adj_all,
    rhs_send, rhs_land, rhs_far, rhs_relay, rhs_own, rhs_all,
    minner_send, minner_land, minner_own, minner_all,
    madj_send, madj_land, madj_far, madj_relay,
    send_sem, recv_sem,
):
    ny, nz, nx = dims
    nq = CORES * nx
    half = ny // 2
    leaf = lax.axis_index("leaf")
    x = lax.axis_index("panel")
    c = lax.rem(leaf, CORES)
    z = lax.rem(lax.div(leaf, CORES), nz)
    y = lax.div(leaf, CORES * nz)
    q = c * nx + x
    y_low = lax.rem(y, half)
    y_base = y - y_low

    def ring(me, count):
        steps = sorted(range(1, count), key=lambda step: -min(step, count - step))
        return [lax.rem(me + step, count) for step in steps]

    def leaf_of(y_at, z_at, c_at):
        return (y_at * nz + z_at) * CORES + c_at

    xs, zs, ys, lows = ring(x, nx), ring(z, nz), ring(y, ny), ring(y_low, half)
    flips = [1 - c]

    def sheet(me, others, base):
        return [
            (y_at * nq + c_at * nx + x_at, (leaf_of(base + y_at, z, c_at), x_at))
            for y_at in others + [me]
            for x_at in xs + [x]
            for c_at in flips + [c]
        ][:-1]

    groups = {
        "q": (nq, q, [(c_at * nx + x_at, (leaf_of(y, z, c_at), x_at)) for x_at in xs + [x] for c_at in flips + [c]][:-1]),
        "y": (ny, y, [(y_at, (leaf_of(y_at, z, c), x)) for y_at in ys]),
        "pair": (half, y_low, [(low, (leaf_of(y_base + low, z, c), x)) for low in lows]),
        "z": (nz, z, [(z_at, (leaf_of(y, z_at, c), x)) for z_at in zs]),
        "plane": (ny * nq, y * nq + q, sheet(y, ys, 0)),
        "half": (half * nq, y_low * nq + q, sheet(y_low, lows, y_base)),
    }
    pending = []

    def push(slot, group, source, landing, peers):
        me = groups[group][1]
        for peer, target in peers:
            pltpu.make_async_remote_copy(
                src_ref=source(peer),
                dst_ref=landing.at[me],
                send_sem=send_sem.at[slot],
                recv_sem=recv_sem.at[slot],
                device_id=target,
                device_id_type=pl.DeviceIdType.MESH,
            ).start()

    def waiter(slot, group, landing):
        count, me, peers = groups[group]
        others = landing.at[pl.ds(0, count - 1)]
        whole = pltpu.make_async_remote_copy(
            src_ref=others,
            dst_ref=others,
            send_sem=send_sem.at[slot],
            recv_sem=recv_sem.at[slot],
            device_id=peers[0][1],
            device_id_type=pl.DeviceIdType.MESH,
        )
        pending.append(whole)
        return whole

    def send(slot, group, source, landing):
        push(slot, group, source, landing, groups[group][2])
        return waiter(slot, group, landing)

    def scatter_sum(slot, group, buffer, landing, between=None):
        me = groups[group][1]
        whole = send(slot, group, lambda peer: buffer.at[peer], landing)
        landing[me] = buffer[me]
        if between is not None:
            between()
        whole.wait_recv()
        return jnp.sum(landing[...], axis=0)

    def gather(slot, group, own, landing, between=None):
        me = groups[group][1]
        whole = send(slot, group, lambda peer: own, landing)
        landing[me] = own[...]
        if between is not None:
            between()
        whole.wait_recv()
        value = landing[...]
        return value.reshape(-1, value.shape[-1])

    leg = nz // 4

    def at(step):
        return lax.rem(z + (step + nz), nz)

    def hop(slot, step, source, landing):
        pltpu.make_async_remote_copy(
            src_ref=source,
            dst_ref=landing,
            send_sem=send_sem.at[slot],
            recv_sem=recv_sem.at[slot],
            device_id=(leaf_of(y, at(step), c), x),
            device_id_type=pl.DeviceIdType.MESH,
        ).start()

    def hop_waiter(slot, landing):
        whole = pltpu.make_async_remote_copy(
            src_ref=landing,
            dst_ref=landing,
            send_sem=send_sem.at[slot],
            recv_sem=recv_sem.at[slot],
            device_id=(leaf_of(y, at(1), c), x),
            device_id_type=pl.DeviceIdType.MESH,
        )
        pending.append(whole)
        return whole

    def ring_sum(far_slot, slot, buffer, land, far, relay):
        for step in range(leg, 0, -1):
            hop(far_slot, step, buffer.at[at(step + leg)], far.at[step - 1])
            if step < leg:
                hop(far_slot, -step, buffer.at[at(-step - leg)], far.at[leg + step - 1])
        for step in range(1, leg):
            hop(slot, step, buffer.at[at(step)], land.at[2 * step - 2])
            hop(slot, -step, buffer.at[at(-step)], land.at[2 * step - 1])
        hop_waiter(far_slot, far).wait_recv()
        relay[0] = buffer[at(leg)] + jnp.sum(far[:leg], axis=0)
        hop(slot, leg, relay.at[0], land.at[2 * leg - 2])
        back = buffer[at(-leg)]
        relay[1] = back + jnp.sum(far[leg:], axis=0) if leg > 1 else back
        hop(slot, -leg, relay.at[1], land.at[2 * leg - 1])
        near_sum = buffer[z]
        hop_waiter(slot, land).wait_recv()
        return near_sum + jnp.sum(land[...], axis=0)

    def ring_gather(far_slot, slot, own, land):
        for step in (leg, -leg):
            hop(far_slot, step, own, land.at[z])
        for step in range(leg - 1, 0, -1):
            hop(slot, step, own, land.at[z])
            hop(slot, -step, own, land.at[z])
        land[z] = own[...]
        hop_waiter(far_slot, land.at[pl.ds(0, 2)]).wait_recv()
        behind, ahead = at(-leg), at(leg)
        for step in range(leg, 0, -1):
            hop(slot, step, land.at[behind], land.at[behind])
            if step < leg:
                hop(slot, -step, land.at[ahead], land.at[ahead])
        hop_waiter(slot, land.at[pl.ds(0, 4 * leg - 3)]).wait_recv()
        value = land[...]
        return value.reshape(-1, value.shape[-1])

    barrier = pltpu.get_barrier_semaphore()
    for name in ("z", "plane"):
        for peer, target in groups[name][2]:
            pl.semaphore_signal(
                barrier, inc=1, device_id=target, device_id_type=pl.DeviceIdType.MESH
            )

    rows = border.shape[0]
    top_rows = top_out.shape[0]
    mid_rows = mid_out.shape[0]
    block = nz * nq * top_rows
    lanes = nz * top_rows
    width = top_factor.shape[1] // nz
    sol_send[...] = solution[...].astype(F32)
    top_send[...] = top_factor[...].astype(F32)

    def regroup(part, owned):
        first = part * ny
        stacked = jnp.concatenate(
            [border[:, (first + b) * block : (first + b + 1) * block] for b in range(ny)], 0
        )
        turned = stacked.astype(F32).T.reshape(block // (nq * owned), nq, owned, ny * rows)
        for q_at in range(nq):
            border_send[part, q_at] = turned[:, q_at].reshape(lanes, ny * rows)

    regroup(0, top_rows)
    pl.semaphore_wait(barrier, ny * nq + nz - 2)

    def columns(ref):
        return lambda peer: ref.at[:, pl.ds(pl.multiple_of(peer * width, width), width)]

    own_columns = pl.ds(pl.multiple_of(z * width, width), width)
    sol_wait = send(0, "q", lambda peer: sol_send, sol_land)
    border_wait = send(1, "q", lambda peer: border_send.at[0, peer], border_land.at[0])
    near = groups["z"][2][::-1]
    early, late = near[: 2 * len(near) // 3], near[2 * len(near) // 3 :]
    push(2, "z", columns(top_send), top_land, near)
    top_wait = waiter(2, "z", top_land)
    regroup(1, mid_rows)
    border_mid_wait = send(18, "q", lambda peer: border_send.at[1, peer], border_land.at[1])
    sol_land[q] = sol_send[...]
    border_land[0, q] = border_send[0, q]
    border_land[1, q] = border_send[1, q]
    sol_blocks[...] = jnp.zeros_like(sol_blocks)
    top_land[z] = top_send[:, own_columns]

    seg = nq * top_rows
    low_half = lax.broadcasted_iota(jnp.int32, (mid_rows, 2 * seg), 1) < seg
    for z_at in range(nz):
        for pair in range(ny // 2):
            tiles = []
            for y_at in (2 * pair, 2 * pair + 1):
                start = (y_at * nz + z_at - z_at % 2) * seg
                tiles.append(coupling[:, start : start + 2 * seg].astype(F32))
            if z_at % 2 == 0:
                tiles[1] = pltpu.roll(tiles[1], seg, 1)
            else:
                tiles[0] = pltpu.roll(tiles[0], seg, 1)
            couple_send[z_at, :, pair * 2 * seg : (pair + 1) * 2 * seg] = jnp.where(
                low_half, tiles[0], tiles[1]
            )

    couple_rows = lambda peer: couple_send.at[peer]
    push(3, "z", couple_rows, couple_land, early)
    couple_wait = waiter(3, "z", couple_land)
    couple_land[z] = couple_send[z]
    mid_send[...] = mid_factor[...].astype(F32)
    mid_land[z] = mid_send[:, own_columns]

    sol_wait.wait_recv()
    columns_out = sol_send.shape[1]
    for source in range(nq):
        part = sol_land[source].astype(BF16)
        for b in range(ny):
            sol_blocks[
                source,
                b * rows : (b + 1) * rows,
                b * columns_out : (b + 1) * columns_out,
            ] = part
    border_wait.wait_recv()

    def loads(part):
        total = None
        for source in range(0, nq, 2):
            left = jnp.concatenate(
                [border_land[part, source], border_land[part, source + 1]], 1
            ).astype(BF16)
            right = sol_blocks[source : source + 2].reshape(2 * ny * rows, -1)
            term = jnp.dot(left, right, preferred_element_type=F32)
            total = term if total is None else total + term
        return [total[:, b * columns_out : (b + 1) * columns_out] for b in range(ny)]

    for b, value in enumerate(loads(0)):
        top_y_send[b] = value
    per_half = ny // half
    top_y_wait = send(5, "y", lambda peer: top_y_send.at[peer], top_y_land)
    top_y_land[y] = top_y_send[y]

    def mid_loads():
        border_mid_wait.wait_recv()
        for b, value in enumerate(loads(1)):
            mid_y_send[
                b // per_half, (b % per_half) * lanes : (b % per_half + 1) * lanes
            ] = value
        push(6, "pair", lambda peer: mid_y_send.at[peer], mid_y_land, groups["pair"][2])
        mid_y_land[y_low] = mid_y_send[y_low]

    mid_y_wait = waiter(6, "pair", mid_y_land)

    def factors_early():
        push(3, "z", couple_rows, couple_land, late)
        push(4, "z", columns(mid_send), mid_land, early)

    def factors_late():
        push(4, "z", columns(mid_send), mid_land, late)

    mid_wait = waiter(4, "z", mid_land)

    top_wait.wait_recv()
    top_t = top_land[...].reshape(nz * top_rows, width)
    top_w = top_t.T.astype(BF16)
    top_t = top_t.astype(BF16)

    top_y_wait.wait_recv()
    load_send[...] = jnp.sum(top_y_land[...], axis=0).reshape(load_send.shape)
    load_own[...] = scatter_sum(7, "z", load_send, load_land)
    top_load = gather(8, "z", load_own, load_all, mid_loads)

    inner_send[...] = dot_split(top_w, top_load).reshape(inner_send.shape)
    inner_own[...] = scatter_sum(9, "plane", inner_send, inner_land, factors_early)
    top_inner = gather(10, "plane", inner_own, inner_all)

    adj_send[...] = dot_split(top_t, top_inner).reshape(adj_send.shape)
    adjoint = scatter_sum(11, "z", adj_send, adj_land)
    adj_own[...] = adjoint
    top_out[...] = adjoint
    top_block = gather(12, "plane", adj_own, adj_all, factors_late)

    couple_wait.wait_recv()
    couple = couple_land[...].reshape(nz * mid_rows, width).astype(BF16)
    mid_y_wait.wait_recv()
    mid_load = jnp.sum(mid_y_land[...], axis=0)
    rhs_send[...] = (mid_load - dot_split(couple, top_block)).reshape(rhs_send.shape)
    rhs_own[...] = ring_sum(13, 19, rhs_send, rhs_land, rhs_far, rhs_relay)
    mid_wait.wait_recv()
    mid_t = mid_land[...].reshape(nz * mid_rows, width)
    mid_w = mid_t.T.astype(BF16)
    mid_t = mid_t.astype(BF16)
    mid_rhs = ring_gather(14, 20, rhs_own, rhs_all)

    minner_send[...] = dot_split(mid_w, mid_rhs).reshape(minner_send.shape)
    minner_own[...] = scatter_sum(15, "half", minner_send, minner_land)
    mid_inner = gather(16, "half", minner_own, minner_all)

    madj_send[...] = dot_split(mid_t, mid_inner).reshape(madj_send.shape)
    mid_out[...] = ring_sum(17, 21, madj_send, madj_land, madj_far, madj_relay)

    for whole in pending:
        whole.wait_send()


def body(dims, border, solution, winv_top, winv_mid, coupling):
    ny, nz, nx = dims
    nq = CORES * nx
    half = ny // 2
    rows, width = border.shape[1:]
    loads = solution.shape[2]
    top_rows = winv_top.shape[1]
    mid_rows = winv_mid.shape[1]
    front = winv_top.shape[0]
    z_width = front // nz

    def buf(*shape):
        return pltpu.VMEM(shape, F32)

    def exchange(count, height):
        return [buf(count, height, loads), buf(count, height, loads)]

    def reduce_gather(count, height):
        return exchange(count, height) + [buf(height, loads), buf(count, height, loads)]

    def two_legs(height):
        leg = nz // 4
        return [buf(count, height, loads) for count in (nz, 2 * leg, 2 * leg - 1, 2)]

    plane = ny * nq
    scratch = (
        [buf(2, nq, nz * top_rows, ny * rows)] * 2
        + [buf(rows, loads), buf(nq, rows, loads)]
        + [pltpu.VMEM((nq, ny * rows, ny * loads), BF16)]
        + [buf(top_rows, front), buf(nz, top_rows, z_width)]
        + [buf(mid_rows, front), buf(nz, mid_rows, z_width)]
        + [buf(nz, mid_rows, z_width)] * 2
        + exchange(ny, nz * top_rows)
        + exchange(half, nz * mid_rows)
        + reduce_gather(nz, top_rows)
        + reduce_gather(plane, z_width // plane)
        + [buf(nz, top_rows, loads)] * 2
        + [buf(top_rows, loads), buf(plane, top_rows, loads)]
        + two_legs(mid_rows)
        + [buf(mid_rows, loads), buf(nz, mid_rows, loads)]
        + reduce_gather(half * nq, z_width // (half * nq))
        + two_legs(mid_rows)
        + [pltpu.SemaphoreType.DMA((22,)), pltpu.SemaphoreType.DMA((22,))]
    )
    vmem = pl.BlockSpec(memory_space=pltpu.VMEM)
    return pl.pallas_call(
        functools.partial(kernel, dims),
        out_shape=(
            jax.ShapeDtypeStruct((top_rows, loads), F32),
            jax.ShapeDtypeStruct((mid_rows, loads), F32),
        ),
        in_specs=[vmem] * 5,
        out_specs=(vmem, vmem),
        scratch_shapes=scratch,
        compiler_params=pltpu.CompilerParams(collective_id=0, has_side_effects=True),
        name="adjoint",
    )(
        border[0],
        solution[0],
        winv_top.T,
        winv_mid.T,
        coupling,
    )


def solution(mesh, chips_y=CHIPS_Y):
    placed = (
        P("leaf", "panel", None),
        P("leaf", "panel", None),
        P(None, ("leaf", "panel")),
        P(None, ("leaf", "panel")),
        P(("leaf", "panel"), None),
    )
    dims = (chips_y, mesh.shape["leaf"] // (CORES * chips_y), mesh.shape["panel"])
    return jax.shard_map(
        functools.partial(body, dims),
        mesh=mesh,
        in_specs=placed,
        out_specs=(P(("leaf", "panel"), None), P(("leaf", "panel"), None)),
        check_vma=False,
    )
```

```python
import functools

import jax
import jax.numpy as jnp
from jax import lax
from jax.experimental import pallas as pl
from jax.experimental.pallas import tpu as pltpu
from jax.sharding import PartitionSpec as P

CHIPS_Y = 4
CORES = 2
F32 = jnp.float32
BF16 = jnp.bfloat16


def dot_split(factor, value):
    high = value.astype(BF16)
    low = (value - high.astype(F32)).astype(BF16)
    return jnp.dot(factor, low, preferred_element_type=F32) + jnp.dot(
        factor, high, preferred_element_type=F32
    )


def kernel(
    dims,
    border, solution, top_factor, mid_factor, coupling,
    top_out, mid_out,
    border_send, border_land, sol_send, sol_land, sol_blocks,
    top_send, top_land, mid_send, mid_land, couple_send, couple_land,
    top_y_send, top_y_land, mid_y_send, mid_y_land,
    load_send, load_land, load_own, load_all,
    inner_send, inner_land, inner_own, inner_all,
    adj_send, adj_land, adj_own, adj_all,
    rhs_send, rhs_land, rhs_own, rhs_all,
    minner_send, minner_land, minner_own, minner_all,
    madj_send, madj_land,
    top_w, top_t, couple_blocks, mid_load, mid_w, mid_t,
    send_sem, recv_sem,
):
    ny, nz, nx = dims
    nq = CORES * nx
    half = ny // 2
    leaf = lax.axis_index("leaf")
    x = lax.axis_index("panel")
    c = lax.rem(leaf, CORES)
    z = lax.rem(lax.div(leaf, CORES), nz)
    y = lax.div(leaf, CORES * nz)
    q = c * nx + x
    y_low = lax.rem(y, half)
    y_base = y - y_low

    def ring(me, count):
        steps = sorted(range(1, count), key=lambda step: -min(step, count - step))
        return [lax.rem(me + step, count) for step in steps]

    def leaf_of(y_at, z_at, c_at):
        return (y_at * nz + z_at) * CORES + c_at

    xs, zs, ys, lows = ring(x, nx), ring(z, nz), ring(y, ny), ring(y_low, half)
    flips = [1 - c]

    def sheet(me, others, base):
        return [
            (y_at * nq + c_at * nx + x_at, (leaf_of(base + y_at, z, c_at), x_at))
            for y_at in others + [me]
            for x_at in xs + [x]
            for c_at in flips + [c]
        ][:-1]

    groups = {
        "q": (nq, q, [(c_at * nx + x_at, (leaf_of(y, z, c_at), x_at)) for x_at in xs + [x] for c_at in flips + [c]][:-1]),
        "y": (ny, y, [(y_at, (leaf_of(y_at, z, c), x)) for y_at in ys]),
        "pair": (half, y_low, [(low, (leaf_of(y_base + low, z, c), x)) for low in lows]),
        "z": (nz, z, [(z_at, (leaf_of(y, z_at, c), x)) for z_at in zs]),
        "plane": (ny * nq, y * nq + q, sheet(y, ys, 0)),
        "half": (half * nq, y_low * nq + q, sheet(y_low, lows, y_base)),
    }
    pending = []

    def push(slot, group, source, landing, peers):
        me = groups[group][1]
        for peer, target in peers:
            pltpu.make_async_remote_copy(
                src_ref=source(peer),
                dst_ref=landing.at[me],
                send_sem=send_sem.at[slot],
                recv_sem=recv_sem.at[slot],
                device_id=target,
                device_id_type=pl.DeviceIdType.MESH,
            ).start()

    def waiter(slot, group, landing):
        count, me, peers = groups[group]
        others = landing.at[pl.ds(0, count - 1)]
        whole = pltpu.make_async_remote_copy(
            src_ref=others,
            dst_ref=others,
            send_sem=send_sem.at[slot],
            recv_sem=recv_sem.at[slot],
            device_id=peers[0][1],
            device_id_type=pl.DeviceIdType.MESH,
        )
        pending.append(whole)
        return whole

    def send(slot, group, source, landing):
        push(slot, group, source, landing, groups[group][2])
        return waiter(slot, group, landing)

    def scatter_sum(slot, group, buffer, landing, between=None):
        me = groups[group][1]
        whole = send(slot, group, lambda peer: buffer.at[peer], landing)
        landing[me] = buffer[me]
        if between is not None:
            between()
        whole.wait_recv()
        return jnp.sum(landing[...], axis=0)

    def gather(slot, group, own, landing, between=None):
        me = groups[group][1]
        whole = send(slot, group, lambda peer: own, landing)
        landing[me] = own[...]
        if between is not None:
            between()
        whole.wait_recv()
        value = landing[...]
        return value.reshape(-1, value.shape[-1])

    barrier = pltpu.get_barrier_semaphore()
    for name in ("z", "plane"):
        for peer, target in groups[name][2]:
            pl.semaphore_signal(
                barrier, inc=1, device_id=target, device_id_type=pl.DeviceIdType.MESH
            )

    rows = border.shape[0]
    top_rows = top_out.shape[0]
    mid_rows = mid_out.shape[0]
    block = nz * nq * top_rows
    lanes = nz * top_rows
    width = top_factor.shape[1] // nz
    sol_send[...] = solution[...].astype(F32)
    top_send[...] = top_factor[...].astype(F32)

    def regroup(part, owned):
        first = part * ny
        stacked = jnp.concatenate(
            [border[:, (first + b) * block : (first + b + 1) * block] for b in range(ny)], 0
        )
        turned = stacked.astype(F32).T.reshape(block // (nq * owned), nq, owned, ny * rows)
        for q_at in range(nq):
            border_send[part, q_at] = turned[:, q_at].reshape(lanes, ny * rows)

    regroup(0, top_rows)
    pl.semaphore_wait(barrier, ny * nq + nz - 2)

    def columns(ref):
        return lambda peer: ref.at[:, pl.ds(pl.multiple_of(peer * width, width), width)]

    own_columns = pl.ds(pl.multiple_of(z * width, width), width)
    sol_wait = send(0, "q", lambda peer: sol_send, sol_land)
    border_wait = send(1, "q", lambda peer: border_send.at[0, peer], border_land.at[0])
    near = groups["z"][2][::-1]
    early, late = near[: 2 * len(near) // 3], near[2 * len(near) // 3 :]
    push(2, "z", columns(top_send), top_land, near)
    top_wait = waiter(2, "z", top_land)
    regroup(1, mid_rows)
    border_mid_wait = send(18, "q", lambda peer: border_send.at[1, peer], border_land.at[1])
    sol_land[q] = sol_send[...]
    border_land[0, q] = border_send[0, q]
    border_land[1, q] = border_send[1, q]
    sol_blocks[...] = jnp.zeros_like(sol_blocks)
    top_land[z] = top_send[:, own_columns]

    seg = nq * top_rows
    low_half = lax.broadcasted_iota(jnp.int32, (mid_rows, 2 * seg), 1) < seg
    for z_at in range(nz):
        for pair in range(ny // 2):
            tiles = []
            for y_at in (2 * pair, 2 * pair + 1):
                start = (y_at * nz + z_at - z_at % 2) * seg
                tiles.append(coupling[:, start : start + 2 * seg].astype(F32))
            if z_at % 2 == 0:
                tiles[1] = pltpu.roll(tiles[1], seg, 1)
            else:
                tiles[0] = pltpu.roll(tiles[0], seg, 1)
            couple_send[z_at, :, pair * 2 * seg : (pair + 1) * 2 * seg] = jnp.where(
                low_half, tiles[0], tiles[1]
            )

    couple_rows = lambda peer: couple_send.at[peer]
    push(3, "z", couple_rows, couple_land, early)
    couple_wait = waiter(3, "z", couple_land)
    couple_land[z] = couple_send[z]
    mid_send[...] = mid_factor[...].astype(F32)
    mid_land[z] = mid_send[:, own_columns]

    sol_wait.wait_recv()
    columns_out = sol_send.shape[1]
    for source in range(nq):
        part = sol_land[source].astype(BF16)
        for b in range(ny):
            sol_blocks[
                source,
                b * rows : (b + 1) * rows,
                b * columns_out : (b + 1) * columns_out,
            ] = part
    border_wait.wait_recv()

    def loads(part):
        total = None
        for source in range(0, nq, 2):
            left = jnp.concatenate(
                [border_land[part, source], border_land[part, source + 1]], 1
            ).astype(BF16)
            right = sol_blocks[source : source + 2].reshape(2 * ny * rows, -1)
            term = jnp.dot(left, right, preferred_element_type=F32)
            total = term if total is None else total + term
        return [total[:, b * columns_out : (b + 1) * columns_out] for b in range(ny)]

    for b, value in enumerate(loads(0)):
        top_y_send[b] = value
    per_half = ny // half
    top_y_wait = send(5, "y", lambda peer: top_y_send.at[peer], top_y_land)
    top_y_land[y] = top_y_send[y]

    def mid_loads():
        border_mid_wait.wait_recv()
        for b, value in enumerate(loads(1)):
            mid_y_send[
                b // per_half, (b % per_half) * lanes : (b % per_half + 1) * lanes
            ] = value
        push(6, "pair", lambda peer: mid_y_send.at[peer], mid_y_land, groups["pair"][2])
        mid_y_land[y_low] = mid_y_send[y_low]

    mid_y_wait = waiter(6, "pair", mid_y_land)

    def factors_early():
        push(3, "z", couple_rows, couple_land, late)
        push(4, "z", columns(mid_send), mid_land, early)

    def factors_late():
        push(4, "z", columns(mid_send), mid_land, late)
        couple_wait.wait_recv()
        couple_blocks[...] = couple_land[...].reshape(nz * mid_rows, width).astype(BF16)
        mid_y_wait.wait_recv()
        mid_load[...] = jnp.sum(mid_y_land[...], axis=0)

    def mid_ready():
        mid_wait.wait_recv()
        blocks = mid_land[...].reshape(nz * mid_rows, width)
        mid_w[...] = blocks.T.astype(BF16)
        mid_t[...] = blocks.astype(BF16)

    mid_wait = waiter(4, "z", mid_land)

    top_wait.wait_recv()
    blocks = top_land[...].reshape(nz * top_rows, width)
    top_w[...] = blocks.T.astype(BF16)
    top_t[...] = blocks.astype(BF16)

    top_y_wait.wait_recv()
    load_send[...] = jnp.sum(top_y_land[...], axis=0).reshape(load_send.shape)
    load_own[...] = scatter_sum(7, "z", load_send, load_land)
    top_load = gather(8, "z", load_own, load_all, mid_loads)

    inner_send[...] = dot_split(top_w[...], top_load).reshape(inner_send.shape)
    inner_own[...] = scatter_sum(9, "plane", inner_send, inner_land, factors_early)
    top_inner = gather(10, "plane", inner_own, inner_all)

    adj_send[...] = dot_split(top_t[...], top_inner).reshape(adj_send.shape)
    adjoint = scatter_sum(11, "z", adj_send, adj_land)
    adj_own[...] = adjoint
    top_out[...] = adjoint
    top_block = gather(12, "plane", adj_own, adj_all, factors_late)

    rhs_send[...] = (mid_load[...] - dot_split(couple_blocks[...], top_block)).reshape(
        rhs_send.shape
    )
    rhs_own[...] = scatter_sum(13, "z", rhs_send, rhs_land, mid_ready)
    mid_rhs = gather(14, "z", rhs_own, rhs_all)

    minner_send[...] = dot_split(mid_w[...], mid_rhs).reshape(minner_send.shape)
    minner_own[...] = scatter_sum(15, "half", minner_send, minner_land)
    mid_inner = gather(16, "half", minner_own, minner_all)

    madj_send[...] = dot_split(mid_t[...], mid_inner).reshape(madj_send.shape)
    mid_out[...] = scatter_sum(17, "z", madj_send, madj_land)

    for whole in pending:
        whole.wait_send()


def body(dims, border, solution, winv_top, winv_mid, coupling):
    ny, nz, nx = dims
    nq = CORES * nx
    half = ny // 2
    rows, width = border.shape[1:]
    loads = solution.shape[2]
    top_rows = winv_top.shape[1]
    mid_rows = winv_mid.shape[1]
    front = winv_top.shape[0]
    z_width = front // nz

    def buf(*shape):
        return pltpu.VMEM(shape, F32)

    def half_buf(*shape):
        return pltpu.VMEM(shape, BF16)

    def exchange(count, height):
        return [buf(count, height, loads), buf(count, height, loads)]

    def reduce_gather(count, height):
        return exchange(count, height) + [buf(height, loads), buf(count, height, loads)]

    plane = ny * nq
    scratch = (
        [buf(2, nq, nz * top_rows, ny * rows)] * 2
        + [buf(rows, loads), buf(nq, rows, loads)]
        + [pltpu.VMEM((nq, ny * rows, ny * loads), BF16)]
        + [buf(top_rows, front), buf(nz, top_rows, z_width)]
        + [buf(mid_rows, front), buf(nz, mid_rows, z_width)]
        + [buf(nz, mid_rows, z_width)] * 2
        + exchange(ny, nz * top_rows)
        + exchange(half, nz * mid_rows)
        + reduce_gather(nz, top_rows)
        + reduce_gather(plane, z_width // plane)
        + [buf(nz, top_rows, loads)] * 2
        + [buf(top_rows, loads), buf(plane, top_rows, loads)]
        + reduce_gather(nz, mid_rows)
        + reduce_gather(half * nq, z_width // (half * nq))
        + exchange(nz, mid_rows)
        + [half_buf(z_width, nz * top_rows), half_buf(nz * top_rows, z_width)]
        + [half_buf(nz * mid_rows, z_width), buf(nz * mid_rows, loads)]
        + [half_buf(z_width, nz * mid_rows), half_buf(nz * mid_rows, z_width)]
        + [pltpu.SemaphoreType.DMA((19,)), pltpu.SemaphoreType.DMA((19,))]
    )
    vmem = pl.BlockSpec(memory_space=pltpu.VMEM)
    return pl.pallas_call(
        functools.partial(kernel, dims),
        out_shape=(
            jax.ShapeDtypeStruct((top_rows, loads), F32),
            jax.ShapeDtypeStruct((mid_rows, loads), F32),
        ),
        in_specs=[vmem] * 5,
        out_specs=(vmem, vmem),
        scratch_shapes=scratch,
        compiler_params=pltpu.CompilerParams(collective_id=0, has_side_effects=True),
        name="adjoint",
    )(
        border[0],
        solution[0],
        winv_top.T,
        winv_mid.T,
        coupling,
    )


def solution(mesh, chips_y=CHIPS_Y):
    placed = (
        P("leaf", "panel", None),
        P("leaf", "panel", None),
        P(None, ("leaf", "panel")),
        P(None, ("leaf", "panel")),
        P(("leaf", "panel"), None),
    )
    dims = (chips_y, mesh.shape["leaf"] // (CORES * chips_y), mesh.shape["panel"])
    return jax.shard_map(
        functools.partial(body, dims),
        mesh=mesh,
        in_specs=placed,
        out_specs=(P(("leaf", "panel"), None), P(("leaf", "panel"), None)),
        check_vma=False,
    )
```

```python
import functools

import jax
import jax.numpy as jnp
from jax import lax
from jax.experimental import pallas as pl
from jax.experimental.pallas import tpu as pltpu
from jax.sharding import PartitionSpec as P

CHIPS_Y = 4
CORES = 2
F32 = jnp.float32
BF16 = jnp.bfloat16


def dot_split(factor, value):
    high = value.astype(BF16)
    low = (value - high.astype(F32)).astype(BF16)
    return jnp.dot(factor, low, preferred_element_type=F32) + jnp.dot(
        factor, high, preferred_element_type=F32
    )


def kernel(
    dims,
    border, solution, top_factor, mid_factor, coupling,
    top_out, mid_out,
    border_send, border_land, sol_send, sol_land, sol_blocks,
    top_send, top_land, mid_send, mid_land, couple_send, couple_land,
    top_y_send, top_y_land, mid_y_send, mid_y_land,
    load_send, load_land, load_own, load_all,
    inner_send, inner_land, inner_own, inner_all,
    adj_send, adj_land, adj_own, adj_all,
    rhs_send, rhs_land, rhs_own, rhs_all,
    minner_send, minner_land, minner_own, minner_all,
    madj_send, madj_land,
    top_w, top_t, couple_blocks, mid_load, mid_w, mid_t,
    send_sem, recv_sem,
):
    ny, nz, nx = dims
    nq = CORES * nx
    half = ny // 2
    leaf = lax.axis_index("leaf")
    x = lax.axis_index("panel")
    c = lax.rem(leaf, CORES)
    z = lax.rem(lax.div(leaf, CORES), nz)
    y = lax.div(leaf, CORES * nz)
    q = c * nx + x
    y_low = lax.rem(y, half)
    y_base = y - y_low

    def ring(me, count):
        steps = sorted(range(1, count), key=lambda step: -min(step, count - step))
        return [lax.rem(me + step, count) for step in steps]

    def leaf_of(y_at, z_at, c_at):
        return (y_at * nz + z_at) * CORES + c_at

    xs, zs, ys, lows = ring(x, nx), ring(z, nz), ring(y, ny), ring(y_low, half)
    flips = [1 - c]

    def sheet(me, others, base):
        return [
            (y_at * nq + c_at * nx + x_at, (leaf_of(base + y_at, z, c_at), x_at))
            for y_at in others + [me]
            for x_at in xs + [x]
            for c_at in flips + [c]
        ][:-1]

    groups = {
        "q": (nq, q, [(c_at * nx + x_at, (leaf_of(y, z, c_at), x_at)) for x_at in xs + [x] for c_at in flips + [c]][:-1]),
        "y": (ny, y, [(y_at, (leaf_of(y_at, z, c), x)) for y_at in ys]),
        "pair": (half, y_low, [(low, (leaf_of(y_base + low, z, c), x)) for low in lows]),
        "z": (nz, z, [(z_at, (leaf_of(y, z_at, c), x)) for z_at in zs]),
        "plane": (ny * nq, y * nq + q, sheet(y, ys, 0)),
        "half": (half * nq, y_low * nq + q, sheet(y_low, lows, y_base)),
    }
    pending = []

    def push(slot, group, source, landing, peers):
        me = groups[group][1]
        for peer, target in peers:
            pltpu.make_async_remote_copy(
                src_ref=source(peer),
                dst_ref=landing.at[me],
                send_sem=send_sem.at[slot],
                recv_sem=recv_sem.at[slot],
                device_id=target,
                device_id_type=pl.DeviceIdType.MESH,
            ).start()

    def waiter(slot, group, landing):
        count, me, peers = groups[group]
        others = landing.at[pl.ds(0, count - 1)]
        whole = pltpu.make_async_remote_copy(
            src_ref=others,
            dst_ref=others,
            send_sem=send_sem.at[slot],
            recv_sem=recv_sem.at[slot],
            device_id=peers[0][1],
            device_id_type=pl.DeviceIdType.MESH,
        )
        pending.append(whole)
        return whole

    def send(slot, group, source, landing):
        push(slot, group, source, landing, groups[group][2])
        return waiter(slot, group, landing)

    def scatter_sum(slot, group, buffer, landing, between=None):
        me = groups[group][1]
        whole = send(slot, group, lambda peer: buffer.at[peer], landing)
        landing[me] = buffer[me]
        if between is not None:
            between()
        whole.wait_recv()
        return jnp.sum(landing[...], axis=0)

    def gather(slot, group, own, landing, between=None):
        me = groups[group][1]
        whole = send(slot, group, lambda peer: own, landing)
        landing[me] = own[...]
        if between is not None:
            between()
        whole.wait_recv()
        value = landing[...]
        return value.reshape(-1, value.shape[-1])

    barrier = pltpu.get_barrier_semaphore()
    for name in ("z", "plane"):
        for peer, target in groups[name][2]:
            pl.semaphore_signal(
                barrier, inc=1, device_id=target, device_id_type=pl.DeviceIdType.MESH
            )

    rows = border.shape[0]
    top_rows = top_out.shape[0]
    mid_rows = mid_out.shape[0]
    block = nz * nq * top_rows
    lanes = nz * top_rows
    width = top_factor.shape[1] // nz
    sol_send[...] = solution[...].astype(F32)
    top_send[...] = top_factor[...].astype(F32)

    def regroup(part, owned):
        first = part * ny
        stacked = jnp.concatenate(
            [border[:, (first + b) * block : (first + b + 1) * block] for b in range(ny)], 0
        )
        turned = stacked.astype(F32).T.reshape(block // (nq * owned), nq, owned, ny * rows)
        for q_at in range(nq):
            border_send[part, q_at] = turned[:, q_at].reshape(lanes, ny * rows)

    regroup(0, top_rows)
    pl.semaphore_wait(barrier, ny * nq + nz - 2)

    def columns(ref):
        return lambda peer: ref.at[:, pl.ds(pl.multiple_of(peer * width, width), width)]

    own_columns = pl.ds(pl.multiple_of(z * width, width), width)
    sol_wait = send(0, "q", lambda peer: sol_send, sol_land)
    border_wait = send(1, "q", lambda peer: border_send.at[0, peer], border_land.at[0])
    near = groups["z"][2][::-1]
    push(2, "z", columns(top_send), top_land, near)
    top_wait = waiter(2, "z", top_land)
    regroup(1, mid_rows)
    border_mid_wait = send(18, "q", lambda peer: border_send.at[1, peer], border_land.at[1])
    sol_land[q] = sol_send[...]
    border_land[0, q] = border_send[0, q]
    border_land[1, q] = border_send[1, q]
    sol_blocks[...] = jnp.zeros_like(sol_blocks)
    top_land[z] = top_send[:, own_columns]

    seg = nq * top_rows
    low_half = lax.broadcasted_iota(jnp.int32, (mid_rows, 2 * seg), 1) < seg
    for z_at in range(nz):
        for pair in range(ny // 2):
            tiles = []
            for y_at in (2 * pair, 2 * pair + 1):
                start = (y_at * nz + z_at - z_at % 2) * seg
                tiles.append(coupling[:, start : start + 2 * seg].astype(F32))
            if z_at % 2 == 0:
                tiles[1] = pltpu.roll(tiles[1], seg, 1)
            else:
                tiles[0] = pltpu.roll(tiles[0], seg, 1)
            couple_send[z_at, :, pair * 2 * seg : (pair + 1) * 2 * seg] = jnp.where(
                low_half, tiles[0], tiles[1]
            )

    couple_rows = lambda peer: couple_send.at[peer]
    push(3, "z", couple_rows, couple_land, near)
    couple_wait = waiter(3, "z", couple_land)
    couple_land[z] = couple_send[z]
    mid_send[...] = mid_factor[...].astype(F32)
    mid_land[z] = mid_send[:, own_columns]

    sol_wait.wait_recv()
    columns_out = sol_send.shape[1]
    for source in range(nq):
        part = sol_land[source].astype(BF16)
        for b in range(ny):
            sol_blocks[
                source,
                b * rows : (b + 1) * rows,
                b * columns_out : (b + 1) * columns_out,
            ] = part
    border_wait.wait_recv()

    def loads(part):
        total = None
        for source in range(0, nq, 2):
            left = jnp.concatenate(
                [border_land[part, source], border_land[part, source + 1]], 1
            ).astype(BF16)
            right = sol_blocks[source : source + 2].reshape(2 * ny * rows, -1)
            term = jnp.dot(left, right, preferred_element_type=F32)
            total = term if total is None else total + term
        return [total[:, b * columns_out : (b + 1) * columns_out] for b in range(ny)]

    for b, value in enumerate(loads(0)):
        top_y_send[b] = value
    per_half = ny // half
    top_y_wait = send(5, "y", lambda peer: top_y_send.at[peer], top_y_land)
    top_y_land[y] = top_y_send[y]

    def mid_loads():
        border_mid_wait.wait_recv()
        for b, value in enumerate(loads(1)):
            mid_y_send[
                b // per_half, (b % per_half) * lanes : (b % per_half + 1) * lanes
            ] = value
        push(6, "pair", lambda peer: mid_y_send.at[peer], mid_y_land, groups["pair"][2])
        mid_y_land[y_low] = mid_y_send[y_low]

    mid_y_wait = waiter(6, "pair", mid_y_land)

    def send_mid_factor():
        push(4, "z", columns(mid_send), mid_land, near)

    def couple_ready():
        couple_wait.wait_recv()
        couple_blocks[...] = couple_land[...].reshape(nz * mid_rows, width).astype(BF16)
        mid_y_wait.wait_recv()
        mid_load[...] = jnp.sum(mid_y_land[...], axis=0)

    def mid_ready():
        mid_wait.wait_recv()
        blocks = mid_land[...].reshape(nz * mid_rows, width)
        mid_w[...] = blocks.T.astype(BF16)
        mid_t[...] = blocks.astype(BF16)

    mid_wait = waiter(4, "z", mid_land)

    top_wait.wait_recv()
    blocks = top_land[...].reshape(nz * top_rows, width)
    top_w[...] = blocks.T.astype(BF16)
    top_t[...] = blocks.astype(BF16)

    top_y_wait.wait_recv()
    load_send[...] = jnp.sum(top_y_land[...], axis=0).reshape(load_send.shape)
    load_own[...] = scatter_sum(7, "z", load_send, load_land)
    top_load = gather(8, "z", load_own, load_all, mid_loads)

    inner_send[...] = dot_split(top_w[...], top_load).reshape(inner_send.shape)
    inner_own[...] = scatter_sum(9, "plane", inner_send, inner_land, send_mid_factor)
    top_inner = gather(10, "plane", inner_own, inner_all)

    adj_send[...] = dot_split(top_t[...], top_inner).reshape(adj_send.shape)
    adjoint = scatter_sum(11, "z", adj_send, adj_land)
    adj_own[...] = adjoint
    top_out[...] = adjoint
    top_block = gather(12, "plane", adj_own, adj_all, couple_ready)

    rhs_send[...] = (mid_load[...] - dot_split(couple_blocks[...], top_block)).reshape(
        rhs_send.shape
    )
    rhs_own[...] = scatter_sum(13, "z", rhs_send, rhs_land, mid_ready)
    mid_rhs = gather(14, "z", rhs_own, rhs_all)

    minner_send[...] = dot_split(mid_w[...], mid_rhs).reshape(minner_send.shape)
    minner_own[...] = scatter_sum(15, "half", minner_send, minner_land)
    mid_inner = gather(16, "half", minner_own, minner_all)

    madj_send[...] = dot_split(mid_t[...], mid_inner).reshape(madj_send.shape)
    mid_out[...] = scatter_sum(17, "z", madj_send, madj_land)

    for whole in pending:
        whole.wait_send()


def body(dims, border, solution, winv_top, winv_mid, coupling):
    ny, nz, nx = dims
    nq = CORES * nx
    half = ny // 2
    rows, width = border.shape[1:]
    loads = solution.shape[2]
    top_rows = winv_top.shape[1]
    mid_rows = winv_mid.shape[1]
    front = winv_top.shape[0]
    z_width = front // nz

    def buf(*shape):
        return pltpu.VMEM(shape, F32)

    def half_buf(*shape):
        return pltpu.VMEM(shape, BF16)

    def exchange(count, height):
        return [buf(count, height, loads), buf(count, height, loads)]

    def reduce_gather(count, height):
        return exchange(count, height) + [buf(height, loads), buf(count, height, loads)]

    plane = ny * nq
    scratch = (
        [buf(2, nq, nz * top_rows, ny * rows)] * 2
        + [buf(rows, loads), buf(nq, rows, loads)]
        + [pltpu.VMEM((nq, ny * rows, ny * loads), BF16)]
        + [buf(top_rows, front), buf(nz, top_rows, z_width)]
        + [buf(mid_rows, front), buf(nz, mid_rows, z_width)]
        + [buf(nz, mid_rows, z_width)] * 2
        + exchange(ny, nz * top_rows)
        + exchange(half, nz * mid_rows)
        + reduce_gather(nz, top_rows)
        + reduce_gather(plane, z_width // plane)
        + [buf(nz, top_rows, loads)] * 2
        + [buf(top_rows, loads), buf(plane, top_rows, loads)]
        + reduce_gather(nz, mid_rows)
        + reduce_gather(half * nq, z_width // (half * nq))
        + exchange(nz, mid_rows)
        + [half_buf(z_width, nz * top_rows), half_buf(nz * top_rows, z_width)]
        + [half_buf(nz * mid_rows, z_width), buf(nz * mid_rows, loads)]
        + [half_buf(z_width, nz * mid_rows), half_buf(nz * mid_rows, z_width)]
        + [pltpu.SemaphoreType.DMA((19,)), pltpu.SemaphoreType.DMA((19,))]
    )
    vmem = pl.BlockSpec(memory_space=pltpu.VMEM)
    return pl.pallas_call(
        functools.partial(kernel, dims),
        out_shape=(
            jax.ShapeDtypeStruct((top_rows, loads), F32),
            jax.ShapeDtypeStruct((mid_rows, loads), F32),
        ),
        in_specs=[vmem] * 5,
        out_specs=(vmem, vmem),
        scratch_shapes=scratch,
        compiler_params=pltpu.CompilerParams(collective_id=0, has_side_effects=True),
        name="adjoint",
    )(
        border[0],
        solution[0],
        winv_top.T,
        winv_mid.T,
        coupling,
    )


def solution(mesh, chips_y=CHIPS_Y):
    placed = (
        P("leaf", "panel", None),
        P("leaf", "panel", None),
        P(None, ("leaf", "panel")),
        P(None, ("leaf", "panel")),
        P(("leaf", "panel"), None),
    )
    dims = (chips_y, mesh.shape["leaf"] // (CORES * chips_y), mesh.shape["panel"])
    return jax.shard_map(
        functools.partial(body, dims),
        mesh=mesh,
        in_specs=placed,
        out_specs=(P(("leaf", "panel"), None), P(("leaf", "panel"), None)),
        check_vma=False,
    )
```

```python
import functools

import jax
import jax.numpy as jnp
from jax import lax
from jax.experimental import pallas as pl
from jax.experimental.pallas import tpu as pltpu
from jax.sharding import PartitionSpec as P

CHIPS_Y = 4
CORES = 2
F32 = jnp.float32
BF16 = jnp.bfloat16


def dot_split(factor, value):
    high = value.astype(BF16)
    low = (value - high.astype(F32)).astype(BF16)
    both = jnp.dot(factor, jnp.concatenate([low, high], 1), preferred_element_type=F32)
    count = value.shape[1]
    return both[:, :count] + both[:, count:]


def kernel(
    dims,
    border, solution, top_factor, mid_factor, coupling,
    top_out, mid_out,
    border_send, border_land, sol_send, sol_land, sol_blocks,
    top_send, top_land, mid_send, mid_land, couple_send, couple_land,
    top_y_send, top_y_land, mid_y_send, mid_y_land,
    load_send, load_land, load_own, load_all,
    inner_send, inner_land, inner_own, inner_all,
    adj_send, adj_land, adj_own, adj_all,
    rhs_send, rhs_land, rhs_own, rhs_all,
    minner_send, minner_land, minner_own, minner_all,
    madj_send, madj_land,
    top_w, top_t, couple_blocks, mid_load, mid_w, mid_t,
    send_sem, recv_sem,
):
    ny, nz, nx = dims
    nq = CORES * nx
    half = ny // 2
    leaf = lax.axis_index("leaf")
    x = lax.axis_index("panel")
    c = lax.rem(leaf, CORES)
    z = lax.rem(lax.div(leaf, CORES), nz)
    y = lax.div(leaf, CORES * nz)
    q = c * nx + x
    y_low = lax.rem(y, half)
    y_base = y - y_low

    def ring(me, count):
        steps = sorted(range(1, count), key=lambda step: -min(step, count - step))
        return [lax.rem(me + step, count) for step in steps]

    def leaf_of(y_at, z_at, c_at):
        return (y_at * nz + z_at) * CORES + c_at

    xs, zs, ys, lows = ring(x, nx), ring(z, nz), ring(y, ny), ring(y_low, half)
    flips = [1 - c]

    def sheet(me, others, base):
        return [
            (y_at * nq + c_at * nx + x_at, (leaf_of(base + y_at, z, c_at), x_at))
            for y_at in others + [me]
            for x_at in xs + [x]
            for c_at in flips + [c]
        ][:-1]

    groups = {
        "q": (nq, q, [(c_at * nx + x_at, (leaf_of(y, z, c_at), x_at)) for x_at in xs + [x] for c_at in flips + [c]][:-1]),
        "y": (ny, y, [(y_at, (leaf_of(y_at, z, c), x)) for y_at in ys]),
        "pair": (half, y_low, [(low, (leaf_of(y_base + low, z, c), x)) for low in lows]),
        "z": (nz, z, [(z_at, (leaf_of(y, z_at, c), x)) for z_at in zs]),
        "plane": (ny * nq, y * nq + q, sheet(y, ys, 0)),
        "half": (half * nq, y_low * nq + q, sheet(y_low, lows, y_base)),
    }
    pending = []

    def push(slot, group, source, landing, peers):
        me = groups[group][1]
        for peer, target in peers:
            pltpu.make_async_remote_copy(
                src_ref=source(peer),
                dst_ref=landing.at[me],
                send_sem=send_sem.at[slot],
                recv_sem=recv_sem.at[slot],
                device_id=target,
                device_id_type=pl.DeviceIdType.MESH,
            ).start()

    def waiter(slot, group, landing):
        count, me, peers = groups[group]
        others = landing.at[pl.ds(0, count - 1)]
        whole = pltpu.make_async_remote_copy(
            src_ref=others,
            dst_ref=others,
            send_sem=send_sem.at[slot],
            recv_sem=recv_sem.at[slot],
            device_id=peers[0][1],
            device_id_type=pl.DeviceIdType.MESH,
        )
        pending.append(whole)
        return whole

    def send(slot, group, source, landing):
        push(slot, group, source, landing, groups[group][2])
        return waiter(slot, group, landing)

    def scatter_sum(slot, group, buffer, landing, between=None):
        me = groups[group][1]
        whole = send(slot, group, lambda peer: buffer.at[peer], landing)
        landing[me] = buffer[me]
        if between is not None:
            between()
        whole.wait_recv()
        return jnp.sum(landing[...], axis=0)

    def gather(slot, group, own, landing, between=None):
        me = groups[group][1]
        whole = send(slot, group, lambda peer: own, landing)
        landing[me] = own[...]
        if between is not None:
            between()
        whole.wait_recv()
        value = landing[...]
        return value.reshape(-1, value.shape[-1])

    barrier = pltpu.get_barrier_semaphore()
    for name in ("z", "plane"):
        for peer, target in groups[name][2]:
            pl.semaphore_signal(
                barrier, inc=1, device_id=target, device_id_type=pl.DeviceIdType.MESH
            )

    rows = border.shape[0]
    top_rows = top_out.shape[0]
    mid_rows = mid_out.shape[0]
    block = nz * nq * top_rows
    lanes = nz * top_rows
    width = top_factor.shape[1] // nz
    sol_send[...] = solution[...].astype(F32)
    top_send[...] = top_factor[...].astype(F32)

    def regroup(part, owned):
        first = part * ny
        stacked = jnp.concatenate(
            [border[:, (first + b) * block : (first + b + 1) * block] for b in range(ny)], 0
        )
        turned = stacked.astype(F32).T.reshape(block // (nq * owned), nq, owned, ny * rows)
        for q_at in range(nq):
            border_send[part, q_at] = turned[:, q_at].reshape(lanes, ny * rows)

    regroup(0, top_rows)
    pl.semaphore_wait(barrier, ny * nq + nz - 2)

    def columns(ref):
        return lambda peer: ref.at[:, pl.ds(pl.multiple_of(peer * width, width), width)]

    own_columns = pl.ds(pl.multiple_of(z * width, width), width)
    sol_wait = send(0, "q", lambda peer: sol_send, sol_land)
    border_wait = send(1, "q", lambda peer: border_send.at[0, peer], border_land.at[0])
    near = groups["z"][2][::-1]
    push(2, "z", columns(top_send), top_land, near)
    top_wait = waiter(2, "z", top_land)
    regroup(1, mid_rows)
    border_mid_wait = send(18, "q", lambda peer: border_send.at[1, peer], border_land.at[1])
    sol_land[q] = sol_send[...]
    border_land[0, q] = border_send[0, q]
    border_land[1, q] = border_send[1, q]
    sol_blocks[...] = jnp.zeros_like(sol_blocks)
    top_land[z] = top_send[:, own_columns]

    seg = nq * top_rows
    low_half = lax.broadcasted_iota(jnp.int32, (mid_rows, 2 * seg), 1) < seg
    for z_at in range(nz):
        for pair in range(ny // 2):
            tiles = []
            for y_at in (2 * pair, 2 * pair + 1):
                start = (y_at * nz + z_at - z_at % 2) * seg
                tiles.append(coupling[:, start : start + 2 * seg].astype(F32))
            if z_at % 2 == 0:
                tiles[1] = pltpu.roll(tiles[1], seg, 1)
            else:
                tiles[0] = pltpu.roll(tiles[0], seg, 1)
            couple_send[z_at, :, pair * 2 * seg : (pair + 1) * 2 * seg] = jnp.where(
                low_half, tiles[0], tiles[1]
            )

    couple_rows = lambda peer: couple_send.at[peer]
    push(3, "z", couple_rows, couple_land, near)
    couple_wait = waiter(3, "z", couple_land)
    couple_land[z] = couple_send[z]
    mid_send[...] = mid_factor[...].astype(F32)
    mid_land[z] = mid_send[:, own_columns]

    sol_wait.wait_recv()
    columns_out = sol_send.shape[1]
    for source in range(nq):
        part = sol_land[source].astype(BF16)
        for b in range(ny):
            sol_blocks[
                source,
                b * rows : (b + 1) * rows,
                b * columns_out : (b + 1) * columns_out,
            ] = part
    border_wait.wait_recv()

    def loads(part):
        total = None
        for source in range(0, nq, 2):
            left = jnp.concatenate(
                [border_land[part, source], border_land[part, source + 1]], 1
            ).astype(BF16)
            right = sol_blocks[source : source + 2].reshape(2 * ny * rows, -1)
            term = jnp.dot(left, right, preferred_element_type=F32)
            total = term if total is None else total + term
        return [total[:, b * columns_out : (b + 1) * columns_out] for b in range(ny)]

    for b, value in enumerate(loads(0)):
        top_y_send[b] = value
    per_half = ny // half
    top_y_wait = send(5, "y", lambda peer: top_y_send.at[peer], top_y_land)
    top_y_land[y] = top_y_send[y]

    def mid_loads():
        border_mid_wait.wait_recv()
        for b, value in enumerate(loads(1)):
            mid_y_send[
                b // per_half, (b % per_half) * lanes : (b % per_half + 1) * lanes
            ] = value
        push(6, "pair", lambda peer: mid_y_send.at[peer], mid_y_land, groups["pair"][2])
        mid_y_land[y_low] = mid_y_send[y_low]

    mid_y_wait = waiter(6, "pair", mid_y_land)

    def send_mid_factor():
        push(4, "z", columns(mid_send), mid_land, near)

    def couple_ready():
        couple_wait.wait_recv()
        couple_blocks[...] = couple_land[...].reshape(nz * mid_rows, width).astype(BF16)
        mid_y_wait.wait_recv()
        mid_load[...] = jnp.sum(mid_y_land[...], axis=0)

    def mid_ready():
        mid_wait.wait_recv()
        blocks = mid_land[...].reshape(nz * mid_rows, width)
        mid_w[...] = blocks.T.astype(BF16)
        mid_t[...] = blocks.astype(BF16)

    mid_wait = waiter(4, "z", mid_land)

    top_wait.wait_recv()
    blocks = top_land[...].reshape(nz * top_rows, width)
    top_w[...] = blocks.T.astype(BF16)
    top_t[...] = blocks.astype(BF16)

    top_y_wait.wait_recv()
    load_send[...] = jnp.sum(top_y_land[...], axis=0).reshape(load_send.shape)
    load_own[...] = scatter_sum(7, "z", load_send, load_land)
    top_load = gather(8, "z", load_own, load_all, mid_loads)

    inner_send[...] = dot_split(top_w[...], top_load).reshape(inner_send.shape)
    inner_own[...] = scatter_sum(9, "plane", inner_send, inner_land, send_mid_factor)
    top_inner = gather(10, "plane", inner_own, inner_all)

    adj_send[...] = dot_split(top_t[...], top_inner).reshape(adj_send.shape)
    adjoint = scatter_sum(11, "z", adj_send, adj_land)
    adj_own[...] = adjoint
    top_out[...] = adjoint
    top_block = gather(12, "plane", adj_own, adj_all, couple_ready)

    rhs_send[...] = (mid_load[...] - dot_split(couple_blocks[...], top_block)).reshape(
        rhs_send.shape
    )
    rhs_own[...] = scatter_sum(13, "z", rhs_send, rhs_land, mid_ready)
    mid_rhs = gather(14, "z", rhs_own, rhs_all)

    minner_send[...] = dot_split(mid_w[...], mid_rhs).reshape(minner_send.shape)
    minner_own[...] = scatter_sum(15, "half", minner_send, minner_land)
    mid_inner = gather(16, "half", minner_own, minner_all)

    madj_send[...] = dot_split(mid_t[...], mid_inner).reshape(madj_send.shape)
    mid_out[...] = scatter_sum(17, "z", madj_send, madj_land)

    for whole in pending:
        whole.wait_send()


def body(dims, border, solution, winv_top, winv_mid, coupling):
    ny, nz, nx = dims
    nq = CORES * nx
    half = ny // 2
    rows, width = border.shape[1:]
    loads = solution.shape[2]
    top_rows = winv_top.shape[1]
    mid_rows = winv_mid.shape[1]
    front = winv_top.shape[0]
    z_width = front // nz

    def buf(*shape):
        return pltpu.VMEM(shape, F32)

    def half_buf(*shape):
        return pltpu.VMEM(shape, BF16)

    def exchange(count, height):
        return [buf(count, height, loads), buf(count, height, loads)]

    def reduce_gather(count, height):
        return exchange(count, height) + [buf(height, loads), buf(count, height, loads)]

    plane = ny * nq
    scratch = (
        [buf(2, nq, nz * top_rows, ny * rows)] * 2
        + [buf(rows, loads), buf(nq, rows, loads)]
        + [pltpu.VMEM((nq, ny * rows, ny * loads), BF16)]
        + [buf(top_rows, front), buf(nz, top_rows, z_width)]
        + [buf(mid_rows, front), buf(nz, mid_rows, z_width)]
        + [buf(nz, mid_rows, z_width)] * 2
        + exchange(ny, nz * top_rows)
        + exchange(half, nz * mid_rows)
        + reduce_gather(nz, top_rows)
        + reduce_gather(plane, z_width // plane)
        + [buf(nz, top_rows, loads)] * 2
        + [buf(top_rows, loads), buf(plane, top_rows, loads)]
        + reduce_gather(nz, mid_rows)
        + reduce_gather(half * nq, z_width // (half * nq))
        + exchange(nz, mid_rows)
        + [half_buf(z_width, nz * top_rows), half_buf(nz * top_rows, z_width)]
        + [half_buf(nz * mid_rows, z_width), buf(nz * mid_rows, loads)]
        + [half_buf(z_width, nz * mid_rows), half_buf(nz * mid_rows, z_width)]
        + [pltpu.SemaphoreType.DMA((19,)), pltpu.SemaphoreType.DMA((19,))]
    )
    vmem = pl.BlockSpec(memory_space=pltpu.VMEM)
    return pl.pallas_call(
        functools.partial(kernel, dims),
        out_shape=(
            jax.ShapeDtypeStruct((top_rows, loads), F32),
            jax.ShapeDtypeStruct((mid_rows, loads), F32),
        ),
        in_specs=[vmem] * 5,
        out_specs=(vmem, vmem),
        scratch_shapes=scratch,
        compiler_params=pltpu.CompilerParams(collective_id=0, has_side_effects=True),
        name="adjoint",
    )(
        border[0],
        solution[0],
        winv_top.T,
        winv_mid.T,
        coupling,
    )


def solution(mesh, chips_y=CHIPS_Y):
    placed = (
        P("leaf", "panel", None),
        P("leaf", "panel", None),
        P(None, ("leaf", "panel")),
        P(None, ("leaf", "panel")),
        P(("leaf", "panel"), None),
    )
    dims = (chips_y, mesh.shape["leaf"] // (CORES * chips_y), mesh.shape["panel"])
    return jax.shard_map(
        functools.partial(body, dims),
        mesh=mesh,
        in_specs=placed,
        out_specs=(P(("leaf", "panel"), None), P(("leaf", "panel"), None)),
        check_vma=False,
    )
```
